512 devices in a mesh: head: 8 (over x, core), wide: 64 (over z, y).
Axes of the slice: x: 4, y: 8, z: 8, core: 2. Of those that a mesh axis runs over, the one named last changes fastest.
Arguments:
- queries: bfloat16 [16384, 2048], P('wide', 'head'), may hold values from -120 to 120
- keys: bfloat16 [16384, 2048], P('wide', 'head'), may hold values from -6 to 6
- values: bfloat16 [16384, 2048], P('wide', 'head'), may hold values from -6 to 6
- out_grad: bfloat16 [16384, 2048], P('wide', 'head'), may hold values from -6 to 6
- qkv_weight: bfloat16 [3, 4096, 2048], P(None, 'wide', 'head'), may hold values from -0.125 to 0.125
- doc_lengths: int32 [32], replicated, may hold values from 1 to 1023, as said below
- image_count: int32 [64], replicated, may hold values 0 or 1
- image_offset: int32 [64], replicated, may hold values from 0 to 192
- slab_owner: int32 [64], replicated, may hold values from 0 to 63, each once
- patch_weight: bfloat16 [256, 4096], P(None, 'head'), may hold values from -0.09375 to 0.09375
- conv_input: bfloat16 [64, 8, 8, 128], P('wide', 'head'), may hold values from -20 to 20
- pre_act: bfloat16 [64, 8, 8, 128], P('wide', 'head'), may hold values from -6 to 6
- kernel_first: float32 [1152, 128], P('wide'), may hold values from -0.1875 to 0.1875
- kernel_second: float32 [1152, 256], P('wide'), may hold values from -0.1875 to 0.1875
- mean_first: float32 [1152, 128], P('wide'), may hold values from -4 to 4
- mean_second: float32 [1152, 256], P('wide'), may hold values from -4 to 4
- square_first: float32 [1152, 128], P('wide'), may hold values from 0.05 to 1
- square_second: float32 [1152, 256], P('wide'), may hold values from 0.05 to 1
Outputs:
- input_grad_t: bfloat16 [4096, 16384], P('head', 'wide')
- new_kernel_first: float32 [1152, 128], P('wide')
- new_kernel_second: float32 [1152, 256], P('wide')
- new_mean_first: float32 [1152, 128], P('wide')
- new_mean_second: float32 [1152, 256], P('wide')
- new_square_first: float32 [1152, 128], P('wide')
- new_square_second: float32 [1152, 256], P('wide')
The draws below stay inside these ranges and needn't reach their ends.
Inputs may be any that keep to these rules, and one draw needn't show every extreme that they name: `doc_lengths`: the first document is longer than 256 and shorter than 768; the last has 1024 minus the first one's length; the documents between come in consecutive pairs whose lengths add up to 1024.
All inputs are finite; a program needn't handle non-finite values.
Results may differ from the reference program's by a relative error of at most 0.013.
Values may be sent and summed in bfloat16 or wider, within the bound.
No kernel may reach another device: no remote copies, remote signals or barrier semaphores. Data moves between devices by JAX's collectives and lax.ppermute only.
A program may use at most 64 MiB of HBM per device.

```python
import math
import jax
import jax.numpy as jnp
from jax import lax

D = 4096
HEADS = 16
HD = 128
TOK_DEV = 256
REACH = 4
PROWS = 8
PCOLS = 8
PCH = 256
CMID = 128
CIN = 128
SEQ = 16384
DOCMAX = 1024
NDOC = 32
IMGTOK = 64
N_HEAD = 8
N_WIDE = 64


def paired_draw(key):
    folded_key = jax.random.fold_in(key, 31)
    first, second = jax.random.split(folded_key)
    width = HEADS * HD
    query = jnp.clip(jax.random.normal(first, (SEQ, width), jnp.float32), -6.0, 6.0)
    keyset = jnp.clip(jax.random.normal(second, (SEQ, width), jnp.float32), -6.0, 6.0)
    return (query, keyset)


def draw_queries(key, part):
    query, keyset = paired_draw(key)
    return query.astype(jnp.bfloat16)


def draw_keys(key, part):
    query, keyset = paired_draw(key)
    return keyset.astype(jnp.bfloat16)


def draw_doc_lengths(key, part):
    folded_key = jax.random.fold_in(key, 7)
    key_one, key_two, key_three = jax.random.split(folded_key, 3)
    pairs = NDOC // 2 - 1
    first = jax.random.randint(key_one, (1,), TOK_DEV + 1, DOCMAX - TOK_DEV, dtype=jnp.int32)
    shorter = jax.random.randint(key_two, (pairs,), 1, DOCMAX, dtype=jnp.int32)
    picked = jax.random.randint(key_three, (), 0, pairs, dtype=jnp.int32)
    shorter = jnp.where(jnp.arange(pairs, dtype=jnp.int32) == picked, 1, shorter)
    middle = jnp.stack([shorter, DOCMAX - shorter], axis=1).reshape(-1)
    return jnp.concatenate([first, middle, DOCMAX - first]).astype(jnp.int32)


def draw_conv_input(key, part):
    folded_key = jax.random.fold_in(key, 11)
    shape = (N_WIDE, PROWS, PCOLS, CIN)
    base = jnp.clip(jax.random.normal(folded_key, shape, jnp.float32), -6.0, 6.0)
    top = 3.2
    channel = jnp.arange(CIN, dtype=jnp.float32) / (CIN - 1)
    scale = jnp.exp(jnp.log(top) * channel)
    return (base * scale).astype(jnp.bfloat16)


def with_ends(entries, stream_key, smallest, high):
    spot = [jax.random.randint(jax.random.fold_in(stream_key, axis), (), 0, length) for axis, length in enumerate(entries.shape)]
    longest = entries.shape.index(max(entries.shape))
    neighbour = spot[:longest] + [(spot[longest] + 1) % entries.shape[longest]] + spot[longest + 1:]
    return entries.at[tuple(spot)].set(smallest).at[tuple(neighbour)].set(high)


def steps_of(own_key, shape, shards, least, high):
    def one(dim, parts):
        draws = jax.random.uniform(jax.random.fold_in(jax.random.fold_in(own_key, 6), dim), (parts,), jnp.float32, least / len(shards), high / len(shards))
        return jnp.repeat(jnp.exp(draws), shape[dim] // parts).reshape((-1,) + (1,) * (len(shape) - dim - 1))

    loudness = one(*shards[0])
    for cut in shards[1:]:
        loudness = loudness * one(*cut)
    return loudness


def centred(key, extent, deviation, most, shards=(), kind=jnp.bfloat16):
    gain = steps_of(key, extent, shards, -0.22, 0.18) if shards else 1.0
    values = jax.random.normal(key, extent, jnp.float32) * deviation * gain
    return jnp.minimum(jnp.maximum(values, -most), most).astype(kind)


def setup_inputs(seed: int = 0) -> dict:
    arg_keys = jax.random.split(jax.random.key(seed), 19)
    queries = draw_queries(jax.random.fold_in(arg_keys[18], 71), 0)
    keys = draw_keys(jax.random.fold_in(arg_keys[18], 71), 0)
    values = centred(arg_keys[2], (SEQ, HEADS * HD), 1.0, 6.0, ((0, 64), (1, 8)))
    out_grad = centred(arg_keys[3], (SEQ, HEADS * HD), 1.0, 6.0, ((0, 64), (1, 8)))
    qkv_weight = centred(arg_keys[4], (3, D, HEADS * HD), (HEADS * HD) ** -0.5, 0.125, ((1, 64), (2, 8)))
    doc_lengths = draw_doc_lengths(jax.random.fold_in(arg_keys[18], 71), 0)
    image_count = with_ends((jax.random.randint(arg_keys[6], (N_WIDE,), 0, 4) < 3).astype(jnp.int32), jax.random.fold_in(arg_keys[6], 1), 0, 1)
    image_offset = with_ends(jax.random.randint(arg_keys[7], (N_WIDE,), 0, TOK_DEV - IMGTOK + 1), jax.random.fold_in(arg_keys[7], 1), 0, TOK_DEV - IMGTOK).astype(jnp.int32)
    slab_owner = jax.random.permutation(arg_keys[8], N_WIDE).astype(jnp.int32)
    patch_weight = centred(arg_keys[9], (PCH, D), D ** -0.5, 0.09375, ((1, 8),))
    conv_input = draw_conv_input(jax.random.fold_in(arg_keys[18], 71), 0)
    pre_act = centred(arg_keys[11], (N_WIDE, PROWS, PCOLS, CMID), 1.0, 6.0, ((0, 64), (1, 8)))
    kernel_first = centred(arg_keys[12], (9 * CIN, CMID), (9 * CIN) ** -0.5, 0.1875, ((0, 64),), jnp.float32)
    kernel_second = centred(arg_keys[13], (9 * CMID, PCH), (9 * CMID) ** -0.5, 0.1875, ((0, 64),), jnp.float32)
    mean_first = centred(arg_keys[14], (9 * CIN, CMID), 0.3, 4.0, ((0, 64),), jnp.float32)
    mean_second = centred(arg_keys[15], (9 * CMID, PCH), 0.3, 4.0, ((0, 64),), jnp.float32)
    square_first = jnp.clip(jnp.exp(math.log(1.0) - 2.9957323 * jax.random.uniform(arg_keys[16], (9 * CIN, CMID), jnp.float32) ** steps_of(arg_keys[16], (9 * CIN, CMID), ((0, 64),), -0.2, 0.2)), 0.05, 1.0)
    square_second = jnp.clip(jnp.exp(math.log(1.0) - 2.9957323 * jax.random.uniform(arg_keys[17], (9 * CMID, PCH), jnp.float32) ** steps_of(arg_keys[17], (9 * CMID, PCH), ((0, 64),), -0.2, 0.2)), 0.05, 1.0)
    return {"queries": queries, "keys": keys, "values": values, "out_grad": out_grad, "qkv_weight": qkv_weight, "doc_lengths": doc_lengths, "image_count": image_count, "image_offset": image_offset, "slab_owner": slab_owner, "patch_weight": patch_weight, "conv_input": conv_input, "pre_act": pre_act, "kernel_first": kernel_first, "kernel_second": kernel_second, "mean_first": mean_first, "mean_second": mean_second, "square_first": square_first, "square_second": square_second}


neg_big = -1e+30
beta_one = 0.9
beta_two = 0.95
adam_eps = 1e-08
learn_rate = 0.02
decay_rate = 0.1
adam_step = 10
norm_eps = 1e-06

def lowered(value):
    return lax.optimization_barrier(value.astype(jnp.bfloat16)).astype(jnp.float32)

def doc_number(places, doc_lengths):
    ends = jnp.cumsum(doc_lengths)
    return lax.optimization_barrier(jnp.sum((places[:, None] >= ends[None, :]).astype(jnp.int32), axis=1))

def image_number(places, image_count, image_offset):
    safe = jnp.clip(places, 0, SEQ - 1)
    block = (safe // TOK_DEV).astype(jnp.int32)
    local = safe - block * TOK_DEV
    present = image_count[block]
    start = image_offset[block]
    inside = (present > 0) & (local >= start) & (local < start + IMGTOK) & (places >= 0)
    return jnp.where(inside, block, -1).astype(jnp.int32)

def allowed_mask(query_places, query_docs, query_images, key_places, key_docs, key_images):
    same_doc = query_docs[:, None] == key_docs[None, :]
    earlier = key_places[None, :] <= query_places[:, None]
    same_image = (query_images[:, None] == key_images[None, :]) & (query_images[:, None] >= 0)
    return same_doc & (earlier | same_image) & (key_places[None, :] >= 0)

def attend_block(query, key_all, value_all, grad_out, allowed):
    scale = 1.0 / math.sqrt(HD)
    rows = query.shape[0]
    count = key_all.shape[0]
    query_h = query.astype(jnp.float32).reshape(rows, -1, HD)
    key_h = key_all.astype(jnp.float32).reshape(count, -1, HD)
    value_h = value_all.astype(jnp.float32).reshape(count, -1, HD)
    grad_h = grad_out.astype(jnp.float32).reshape(rows, -1, HD)
    scores = jnp.einsum('qhd,khd->hqk', query_h, key_h) * scale
    scores = jnp.where(allowed[None], scores, neg_big)
    top = lax.optimization_barrier(jnp.max(scores, axis=-1, keepdims=True))
    expo = jnp.where(allowed[None], jnp.exp(scores - top), 0.0)
    prob = expo / lax.optimization_barrier(jnp.sum(expo, axis=-1, keepdims=True))
    prob_low = lowered(prob)
    output = jnp.einsum('hqk,khd->qhd', prob_low, value_h)
    delta = jnp.einsum('qhd,qhd->hq', grad_h, output)
    dprob = jnp.einsum('qhd,khd->hqk', grad_h, value_h)
    dscore = lowered(prob * (dprob - delta[:, :, None]))
    dquery = jnp.einsum('hqk,khd->qhd', dscore, key_h) * scale
    dkey = jnp.einsum('hqk,qhd->khd', dscore, query_h) * scale
    dvalue = jnp.einsum('hqk,qhd->khd', prob_low, grad_h)
    return (dquery.reshape(rows, -1), dkey.reshape(count, -1), dvalue.reshape(count, -1))

def adam_update(param, mean, square, grad):
    new_mean = beta_one * mean + (1.0 - beta_one) * grad
    new_square = beta_two * square + (1.0 - beta_two) * grad * grad
    fixed_mean = new_mean / (1.0 - beta_one ** adam_step)
    fixed_square = new_square / (1.0 - beta_two ** adam_step)
    new_param = param - learn_rate * (fixed_mean / (jnp.sqrt(fixed_square) + adam_eps) + decay_rate * param)
    return (new_param, new_mean, new_square)

def reference(queries, keys, values, out_grad, qkv_weight, doc_lengths, image_count, image_offset, slab_owner, patch_weight, conv_input, pre_act, kernel_first, kernel_second, mean_first, mean_second, square_first, square_second):
    head_width = HEADS * HD
    front = REACH * TOK_DEV
    window = (REACH + 1) * TOK_DEV
    places = jnp.arange(SEQ, dtype=jnp.int32)
    docs = doc_number(places, doc_lengths)
    images = image_number(places, image_count, image_offset)
    pad_places = jnp.arange(-front, SEQ, dtype=jnp.int32)
    pad_docs = jnp.concatenate([jnp.full((front,), -1, jnp.int32), docs])
    pad_images = jnp.concatenate([jnp.full((front,), -1, jnp.int32), images])
    zeros_front = jnp.zeros((front, head_width), jnp.bfloat16)
    pad_keys = jnp.concatenate([zeros_front, keys], axis=0)
    pad_values = jnp.concatenate([zeros_front, values], axis=0)

    def one_block(carry, block):
        key_acc, value_acc = carry
        begin = (block * TOK_DEV).astype(jnp.int32)
        query = lax.dynamic_slice_in_dim(queries, begin, TOK_DEV, 0)
        grad_out = lax.dynamic_slice_in_dim(out_grad, begin, TOK_DEV, 0)
        key_all = lax.dynamic_slice_in_dim(pad_keys, begin, window, 0)
        value_all = lax.dynamic_slice_in_dim(pad_values, begin, window, 0)
        allowed = allowed_mask(lax.dynamic_slice_in_dim(places, begin, TOK_DEV, 0), lax.dynamic_slice_in_dim(docs, begin, TOK_DEV, 0), lax.dynamic_slice_in_dim(images, begin, TOK_DEV, 0), lax.dynamic_slice_in_dim(pad_places, begin, window, 0), lax.dynamic_slice_in_dim(pad_docs, begin, window, 0), lax.dynamic_slice_in_dim(pad_images, begin, window, 0))
        dquery, dkey, dvalue = attend_block(query, key_all, value_all, grad_out, allowed)
        key_acc = lax.dynamic_update_slice_in_dim(key_acc, lax.dynamic_slice_in_dim(key_acc, begin, window, 0) + dkey, begin, 0)
        value_acc = lax.dynamic_update_slice_in_dim(value_acc, lax.dynamic_slice_in_dim(value_acc, begin, window, 0) + dvalue, begin, 0)
        return ((key_acc, value_acc), dquery)
    start_acc = jnp.zeros((front + SEQ, head_width), jnp.float32)
    (key_acc, value_acc), dqueries = lax.scan(one_block, (start_acc, start_acc), jnp.arange(N_WIDE, dtype=jnp.int32))
    grad_query = dqueries.reshape(SEQ, head_width).astype(jnp.bfloat16)
    grad_key = key_acc[front:].astype(jnp.bfloat16)
    grad_value = value_acc[front:].astype(jnp.bfloat16)
    grads = [grad_query, grad_key, grad_value]
    group_width = head_width // N_HEAD
    total = jnp.zeros((D, SEQ), jnp.float32)
    for group in range(N_HEAD):
        low_col = group * group_width
        partial_value = jnp.zeros((D, SEQ), jnp.float32)
        for proj in range(3):
            partial_value = partial_value + jnp.dot(qkv_weight[proj][:, low_col:low_col + group_width], grads[proj][:, low_col:low_col + group_width].T, preferred_element_type=jnp.float32)
        total = total + lowered(partial_value)
    input_grad_t = total.astype(jnp.bfloat16)
    patch_grad = lax.dot_general(input_grad_t, patch_weight, (((0,), (1,)), ((), ())), preferred_element_type=jnp.float32).astype(jnp.bfloat16)

    def take_image(block):
        begin = (block * TOK_DEV + image_offset[block]).astype(jnp.int32)
        return lax.dynamic_slice_in_dim(patch_grad, begin, IMGTOK, 0) * image_count[block].astype(jnp.bfloat16)
    segments = jax.vmap(take_image)(jnp.arange(N_WIDE, dtype=jnp.int32))
    incoming = jnp.zeros((N_WIDE, IMGTOK, PCH), jnp.bfloat16).at[slab_owner].set(segments)
    grad_img = incoming.astype(jnp.float32).reshape(N_WIDE, PROWS, PCOLS, PCH)
    act = lowered(jax.nn.silu(pre_act.astype(jnp.float32)))
    frame = ((0, 0), (1, 1), (1, 1), (0, 0))
    input_pad = jnp.pad(conv_input.astype(jnp.float32), frame)
    act_pad = jnp.pad(act, frame)
    grad_pad = jnp.pad(grad_img, frame)
    kernel_low = lowered(kernel_second).reshape(CMID, 9, PCH)
    second_list = []
    dact = jnp.zeros((N_WIDE, PROWS, PCOLS, CMID), jnp.float32)
    for row_shift in range(3):
        for col_shift in range(3):
            offset = row_shift * 3 + col_shift
            piece = act_pad[:, row_shift:row_shift + PROWS, col_shift:col_shift + PCOLS]
            second_list.append(jnp.einsum('nrcm,nrcp->mp', piece, grad_img))
            moved = grad_pad[:, 2 - row_shift:2 - row_shift + PROWS, 2 - col_shift:2 - col_shift + PCOLS]
            dact = dact + jnp.einsum('nrcp,mp->nrcm', moved, kernel_low[:, offset])
    grad_second = jnp.stack(second_list, axis=1).reshape(9 * CMID, PCH)
    pre_full = pre_act.astype(jnp.float32)
    sig = jax.nn.sigmoid(pre_full)
    dpre = lowered(dact * sig * (1.0 + pre_full * (1.0 - sig)))
    first_list = []
    for row_shift in range(3):
        for col_shift in range(3):
            piece = input_pad[:, row_shift:row_shift + PROWS, col_shift:col_shift + PCOLS]
            first_list.append(jnp.einsum('nrci,nrcm->im', piece, dpre))
    grad_first = jnp.stack(first_list, axis=1).reshape(9 * CIN, CMID)
    squares = jnp.sum(grad_first * grad_first) + jnp.sum(grad_second * grad_second)
    limit = 0.5 * math.sqrt(9 * CIN * CMID + 9 * CMID * PCH)
    factor = jnp.minimum(1.0, limit / (jnp.sqrt(squares) + norm_eps))
    kernel_one, mean_one, square_one = adam_update(kernel_first, mean_first, square_first, grad_first * factor)
    kernel_two, mean_two, square_two = adam_update(kernel_second, mean_second, square_second, grad_second * factor)
    return (input_grad_t, kernel_one, kernel_two, mean_one, mean_two, square_one, square_two)
```

```python
import math

import jax
import jax.numpy as jnp
from jax import lax
from jax.experimental import pallas as pl
from jax.experimental.pallas import tpu as pltpu
from jax.sharding import Mesh
from jax.sharding import PartitionSpec as P

HD = 128
REACH = 4
PROWS = 8
PCOLS = 8
PCH = 256
CMID = 128
CIN = 128
IMGTOK = 64
TOK = 256
WIDE = ("z", "yh", "yl")
LANES = 896

neg_big = -1e30
beta_one = 0.9
beta_two = 0.95
adam_eps = 1e-08
learn_rate = 0.02
decay_rate = 0.1
adam_step = 10
norm_eps = 1e-06
scale = 1.0 / math.sqrt(HD)

f32 = jnp.float32
bf16 = jnp.bfloat16


def nt(a, b):
    return lax.dot_general(a, b, (((1,), (1,)), ((), ())), preferred_element_type=f32)


def nn(a, b):
    return lax.dot_general(a, b, (((1,), (0,)), ((), ())), preferred_element_type=f32)


def tn(a, b):
    return lax.dot_general(a, b, (((0,), (0,)), ((), ())), preferred_element_type=f32)


def head_cols(h):
    return slice(h * HD, (h + 1) * HD)


def masked_scores(key_h, query_h, low, high, shift):
    scores = nt(key_h, query_h) * scale
    place = lax.broadcasted_iota(jnp.int32, scores.shape, 0) - shift
    seen = place >= low
    if high is not None:
        seen = seen & (place <= high)
    return jnp.where(seen, scores, neg_big)


def stats_kernel(meta, q, g, k0, v0, b1, b2, b3, b4, stats, scores_ref):
    near = [b1, b2, b3, b4]
    low = meta[1:2, :]
    high = meta[0:1, :]
    rows = []
    for h in range(2):
        cols = head_cols(h)
        query_h = q[:, cols]
        grad_h = g[:, cols]
        top = None
        for d in range(REACH + 1):
            key_h = k0[:, cols] if d == 0 else near[d - 1][0, :, cols]
            s = masked_scores(key_h, query_h, low, high if d == 0 else None, d * TOK)
            scores_ref[d] = s
            best = jnp.max(s, axis=0, keepdims=True)
            top = best if top is None else jnp.maximum(top, best)
        total = jnp.zeros((1, TOK), f32)
        for d in range(REACH + 1):
            e = jnp.exp(scores_ref[d] - top)
            scores_ref[d] = e
            total = total + jnp.sum(e, axis=0, keepdims=True)
        inverse = 1.0 / total
        delta = jnp.zeros((1, TOK), f32)
        for d in range(REACH + 1):
            value_h = v0[:, cols] if d == 0 else near[d - 1][1, :, cols]
            low_p = (scores_ref[d] * inverse).astype(bf16).astype(f32)
            delta = delta + jnp.sum(low_p * nt(value_h, grad_h), axis=0, keepdims=True)
        rows.append((top, inverse, delta))
    for h in range(2):
        for n in range(3):
            stats[3 * h + n : 3 * h + n + 1, :] = rows[h][n]
    stats[6:8, :] = jnp.zeros((2, TOK), f32)


def own_kernel(meta, stats, q, g, k0, v0, b1, b2, b3, b4, dq, dk, dv):
    near = [b1, b2, b3, b4]
    low = meta[1:2, :]
    high = meta[0:1, :]
    for h in range(2):
        cols = head_cols(h)
        query_h = q[:, cols]
        grad_h = g[:, cols]
        top = stats[3 * h : 3 * h + 1, :]
        inverse = stats[3 * h + 1 : 3 * h + 2, :]
        delta = stats[3 * h + 2 : 3 * h + 3, :]
        acc = jnp.zeros((TOK, HD), f32)
        for d in range(REACH + 1):
            key_h = k0[:, cols] if d == 0 else near[d - 1][0, :, cols]
            value_h = v0[:, cols] if d == 0 else near[d - 1][1, :, cols]
            s = masked_scores(key_h, query_h, low, high if d == 0 else None, d * TOK)
            prob = jnp.exp(s - top) * inverse
            ds = (prob * (nt(value_h, grad_h) - delta)).astype(bf16)
            acc = acc + tn(ds, key_h)
            if d == 0:
                dk[:, cols] = nn(ds, query_h)
                dv[:, cols] = nn(prob.astype(bf16), grad_h)
        dq[:, cols] = (acc * scale).astype(bf16)


def later_kernel(
    start, meta, k0, v0, a1, a2, a3, a4, s1, s2, s3, s4, dq, dk, dv, out, image
):
    later = [a1, a2, a3, a4]
    stats = [s1, s2, s3, s4]
    for h in range(2):
        cols = head_cols(h)
        key_h = k0[:, cols]
        value_h = v0[:, cols]
        dkey = dk[:, cols]
        dvalue = dv[:, cols]
        for d in range(1, REACH + 1):
            query_h = later[d - 1][0, :, cols]
            grad_h = later[d - 1][1, :, cols]
            row = stats[d - 1]
            low = meta[1 + d : 2 + d, :]
            s = masked_scores(key_h, query_h, low, None, 0)
            prob = jnp.exp(s - row[3 * h : 3 * h + 1, :]) * row[3 * h + 1 : 3 * h + 2, :]
            ds = (prob * (nt(value_h, grad_h) - row[3 * h + 2 : 3 * h + 3, :])).astype(bf16)
            dkey = dkey + nn(ds, query_h)
            dvalue = dvalue + nn(prob.astype(bf16), grad_h)
        out[1, :, cols] = (dkey * scale).astype(bf16)
        out[2, :, cols] = dvalue.astype(bf16)
    out[0] = dq[...]
    at = start[0]
    row = lax.broadcasted_iota(jnp.int32, (IMGTOK, TOK), 0) + at
    col = lax.broadcasted_iota(jnp.int32, (IMGTOK, TOK), 1)
    pick = jnp.where(row == col, 1.0, 0.0).astype(bf16)
    for n in range(3):
        image[n] = nn(pick, out[n]).astype(bf16)


def patch_kernel(w, g0, g1, pw, out, acc):
    step = pl.program_id(0)

    @pl.when(step == 0)
    def _():
        acc[...] = jnp.zeros_like(acc)

    for n, g in enumerate((g0, g1)):
        t = jnp.zeros((IMGTOK, TOK), f32)
        for p in range(3):
            t = t + nt(g[p], w[0, :, p].reshape(TOK, TOK))
        acc[n] = acc[n] + nt(t.astype(bf16), pw[0])

    @pl.when(step == pl.num_programs(0) - 1)
    def _():
        out[...] = acc[...].astype(bf16)


def grad_kernel(w, g0, g1, out):
    for n, g in enumerate((g0, g1)):
        t = jnp.zeros((TOK, TOK), f32)
        for p in range(3):
            t = t + nt(w[0, :, p].reshape(TOK, TOK), g[p])
        out[0, :, n * TOK : (n + 1) * TOK] = t.astype(bf16)


def conv_kernel(scalars, pieces, k2, slope, left, out):
    head = scalars[0]
    present = scalars[1].astype(f32)
    total = jnp.zeros((IMGTOK, PCH), f32)
    for n in range(pieces.shape[0]):
        total = total + pieces[n].astype(f32)
    incoming = (total * present).astype(bf16)
    q = lax.broadcasted_iota(jnp.int32, (IMGTOK, IMGTOK), 0)
    p = lax.broadcasted_iota(jnp.int32, (IMGTOK, IMGTOK), 1)
    shifts = []
    for o in range(9):
        dr, dc = o // 3 - 1, o % 3 - 1
        hit = ((p >> 3) == (q >> 3) - dr) & ((p & 7) == (q & 7) - dc)
        shifts.append(jnp.where(hit, 1.0, 0.0).astype(bf16))
    dact = jnp.zeros((IMGTOK, 16), f32)
    for o in range(9):
        dact = dact + nt(nn(shifts[o], incoming).astype(bf16), k2[o])
    dpre = (dact * slope[...]).astype(bf16)
    ch = lax.broadcasted_iota(jnp.int32, (PCH, LANES), 0)
    lane = lax.broadcasted_iota(jnp.int32, (PCH, LANES), 1)
    spread = jnp.where((lane < 576) & ((lane & 31) == ch - 32 * head), 1.0, 0.0).astype(bf16)
    ch = lax.broadcasted_iota(jnp.int32, (16, LANES), 0)
    lane = lax.broadcasted_iota(jnp.int32, (16, LANES), 1)
    spread_first = jnp.where((lane >= 576) & ((lane & 15) == ch), 1.0, 0.0).astype(bf16)
    both = (nn(incoming, spread) + nn(dpre, spread_first)).astype(bf16)
    lane = lax.broadcasted_iota(jnp.int32, (IMGTOK, LANES), 1)
    second = jnp.where(lane >= 288, lane - 288, lane) >> 5
    first = (jnp.where(lane >= 720, lane - 720, lane - 576)) >> 4
    which = jnp.where(lane < 576, second, first)
    moved = jnp.zeros((IMGTOK, LANES), f32)
    zero = jnp.zeros((IMGTOK, LANES), bf16)
    for o in range(9):
        moved = moved + nn(shifts[o], jnp.where(which == o, both, zero))
    moved = moved.astype(bf16)
    ends = (0, 288, 576, 720, 864)
    result = jnp.zeros((IMGTOK, LANES), f32)
    for n in range(4):
        part = jnp.where((lane >= ends[n]) & (lane < ends[n + 1]), moved, zero)
        result = result + nn(left[n], part)
    out[...] = result.astype(bf16)


def whole(space=None):
    return pl.BlockSpec(memory_space=pltpu.VMEM if space is None else space)


def on_chip(kernel, shapes, count, scratch=(), scalars=0):
    return pl.pallas_call(
        kernel,
        out_shape=shapes,
        in_specs=[whole(pltpu.SMEM)] * scalars + [whole()] * (count - scalars),
        out_specs=jax.tree.map(lambda _: whole(), shapes),
        scratch_shapes=list(scratch),
    )


def spec_of(shape, dtype):
    return jax.ShapeDtypeStruct(shape, dtype)


def pick_entry(lookup, wanted):
    return jnp.sum(jnp.where(jnp.arange(lookup.shape[0]) == wanted, lookup, 0))


def passed_along(block, axis, distance):
    devices = range(lax.axis_size(axis))
    route = [(i - distance, i) for i in devices if i - distance in devices]
    return lax.ppermute(block, axis, route)


def swapped(value):
    return lax.ppermute(value, "yl", [(0, 1), (1, 0)])


def exchanged(pieces, axis):
    return lax.all_to_all(pieces, axis, split_axis=0, concat_axis=0, tiled=True)


def sent_to_all(value, axis):
    return exchanged(jnp.broadcast_to(value, (lax.axis_size(axis), *value.shape)), axis)


def adam_update(param, mean, square, grad):
    new_mean = beta_one * mean + (1.0 - beta_one) * grad
    new_square = beta_two * square + (1.0 - beta_two) * grad * grad
    fixed_mean = new_mean / (1.0 - beta_one**adam_step)
    fixed_square = new_square / (1.0 - beta_two**adam_step)
    new_param = param - learn_rate * (
        fixed_mean / (jnp.sqrt(fixed_square) + adam_eps) + decay_rate * param
    )
    return (new_param, new_mean, new_square)


def seen_range(block, doc_lengths, image_count, image_offset):
    index = jnp.arange(doc_lengths.shape[0])
    ends = jnp.sum(jnp.where(index[None, :] <= index[:, None], doc_lengths[None, :], 0), axis=1)
    starts = ends - doc_lengths
    base = block * TOK
    places = base + jnp.arange((REACH + 1) * TOK, dtype=jnp.int32)
    begun = starts[:, None] <= places[None, :]
    low = jnp.max(jnp.where(begun, starts[:, None], 0), axis=0)
    own = places[:TOK]
    over = ends[:, None] > own[None, :]
    doc_end = jnp.min(jnp.where(over, ends[:, None], jnp.int32(1 << 30)), axis=0)
    present = pick_entry(image_count, block)
    offset = pick_entry(image_offset, block)
    local = own - base
    inside = (present > 0) & (local >= offset) & (local < offset + IMGTOK)
    high = jnp.where(
        inside, jnp.maximum(own, jnp.minimum(base + offset + IMGTOK, doc_end) - 1), own
    )
    rows = [high[None], low.reshape(REACH + 1, TOK), jnp.zeros((2, TOK), jnp.int32) + base]
    return jnp.concatenate(rows, axis=0) - base, present, offset


def shards(
    queries,
    keys,
    values,
    out_grad,
    qkv_weight,
    doc_lengths,
    image_count,
    image_offset,
    slab_owner,
    patch_weight,
    conv_input,
    pre_act,
    kernel_first,
    kernel_second,
    mean_first,
    mean_second,
    square_first,
    square_second,
):
    device_index = lax.axis_index(WIDE)
    head_index = lax.axis_index("head")
    side = lax.axis_index("yl")

    before = jnp.stack([keys, values])
    after = jnp.stack([queries, out_grad])
    earlier, later = [], []
    for _ in range(REACH):
        before = passed_along(before, WIDE, 1)
        after = passed_along(after, WIDE, -1)
        earlier.append(before)
        later.append(after)

    meta, present, offset = seen_range(device_index, doc_lengths, image_count, image_offset)

    weights = lax.all_gather(qkv_weight, ("z", "yh"), axis=0).reshape(8, 4, 3, 64, TOK)
    half_patch = lax.dynamic_index_in_dim(
        patch_weight.reshape(PCH, 4, 2, 64), side, 2, keepdims=False
    ).reshape(PCH, TOK)
    patch_half = lax.all_gather(half_patch, "head", axis=0)
    rows = jnp.concatenate([conv_input.reshape(PCOLS, CIN), pre_act.reshape(PCOLS, CMID)], axis=1)
    slots = lax.all_gather(rows, WIDE, axis=0)
    slot = pick_entry(slab_owner, device_index)
    my_rows = lax.dynamic_index_in_dim(slots, slot, 0, keepdims=False)
    picture = lax.all_gather(my_rows, "head", axis=0).reshape(IMGTOK, CIN + CMID)
    kernel_all = lax.all_gather(kernel_second.astype(bf16), WIDE, axis=0)
    kernel_mine = lax.dynamic_slice_in_dim(
        kernel_all.reshape(CMID, 9, PCH), head_index * 16, 16, 0
    ).transpose(1, 0, 2)

    conv_img = picture[:, :CIN]
    pre_img = picture[:, CIN:].astype(f32)
    act = jax.nn.silu(pre_img).astype(bf16)
    left = jnp.concatenate([act.T.reshape(64, 2, 64), conv_img.T.reshape(64, 2, 64)], axis=1)
    left = left.transpose(1, 0, 2)
    sig = jax.nn.sigmoid(pre_img)
    slope = sig * (1.0 + pre_img * (1.0 - sig))
    slope = lax.dynamic_slice_in_dim(slope, head_index * 16, 16, 1)

    stats = on_chip(
        stats_kernel,
        spec_of((8, TOK), f32),
        9,
        [pltpu.VMEM((REACH + 1, TOK, TOK), f32)],
    )(meta, queries, out_grad, keys, values, *earlier)
    stats_later = [passed_along(stats, WIDE, -d) for d in range(1, REACH + 1)]
    dq, dk, dv = on_chip(
        own_kernel,
        (spec_of((TOK, TOK), bf16), spec_of((TOK, TOK), f32), spec_of((TOK, TOK), f32)),
        10,
    )(meta, stats, queries, out_grad, keys, values, *earlier)
    grads, image_grads = on_chip(
        later_kernel,
        (spec_of((3, TOK, TOK), bf16), spec_of((3, IMGTOK, TOK), bf16)),
        15,
        scalars=1,
    )(offset[None], meta, keys, values, *later, *stats_later, dq, dk, dv)

    image_other = swapped(image_grads)
    grads_other = swapped(grads)

    def in_order(own, other):
        return jnp.where(side == 0, own, other), jnp.where(side == 0, other, own)

    weight_block = pl.BlockSpec((1, 4, 3, 64, TOK), lambda i: (i, 0, 0, 0, 0))

    def fixed(*shape):
        return pl.BlockSpec(shape, lambda i: (0,) * len(shape))

    patch_part = pl.pallas_call(
        patch_kernel,
        out_shape=spec_of((2, IMGTOK, PCH), bf16),
        grid=(8,),
        in_specs=[
            weight_block,
            fixed(3, IMGTOK, TOK),
            fixed(3, IMGTOK, TOK),
            pl.BlockSpec((1, PCH, TOK), lambda i: (i, 0, 0)),
        ],
        out_specs=fixed(2, IMGTOK, PCH),
        scratch_shapes=[pltpu.VMEM((2, IMGTOK, PCH), f32)],
    )(weights, *in_order(image_grads, image_other), patch_half)
    pieces = exchanged(
        jnp.broadcast_to(patch_part, (8, 2, IMGTOK, PCH)).reshape(16, IMGTOK, PCH), ("head", "yl")
    )

    flags = jnp.stack([head_index.astype(jnp.int32), present.astype(jnp.int32)])
    partial = on_chip(conv_kernel, spec_of((64, LANES), bf16), 5, scalars=1)(
        flags, pieces, kernel_mine, slope, left
    )

    halves = pl.pallas_call(
        grad_kernel,
        out_shape=spec_of((8, TOK, 2 * TOK), bf16),
        grid=(8,),
        in_specs=[weight_block, fixed(3, TOK, TOK), fixed(3, TOK, TOK)],
        out_specs=pl.BlockSpec((1, TOK, 2 * TOK), lambda i: (i, 0, 0)),
    )(weights, *in_order(grads, grads_other))
    summed = jnp.sum(exchanged(halves, "head").astype(f32), axis=0).astype(bf16)
    mine, theirs = in_order(summed[:, :TOK], summed[:, TOK:])
    arrived = swapped(theirs)
    even, odd = in_order(mine, arrived)
    input_grad_t = jnp.stack([even.reshape(4, 64, TOK), odd.reshape(4, 64, TOK)], axis=1)
    input_grad_t = input_grad_t.reshape(512, TOK)

    owned = exchanged(partial.reshape(64, 7, 128), WIDE)
    owned = jnp.sum(owned.astype(f32), axis=0)
    squares = jnp.broadcast_to(jnp.sum(owned * owned), (1, 128))
    squares = jnp.sum(sent_to_all(squares, WIDE), axis=0)
    together = sent_to_all(jnp.concatenate([owned, squares], axis=0), "head")
    total = jnp.sum(together[:, 7, 0])
    columns = together[:, :7].reshape(8, LANES)
    grad_second = (
        columns[:, :576].reshape(8, 2, 9, 32).transpose(1, 2, 0, 3).reshape(18, PCH)
    )
    grad_first = (
        columns[:, 576:864].reshape(8, 2, 9, 16).transpose(1, 2, 0, 3).reshape(18, CMID)
    )
    limit = 0.5 * math.sqrt(9 * CIN * CMID + 9 * CMID * PCH)
    factor = jnp.minimum(1.0, limit / (jnp.sqrt(total) + norm_eps))
    kernel_one, mean_one, square_one = adam_update(
        kernel_first, mean_first, square_first, grad_first * factor
    )
    kernel_two, mean_two, square_two = adam_update(
        kernel_second, mean_second, square_second, grad_second * factor
    )
    return (input_grad_t, kernel_one, kernel_two, mean_one, mean_two, square_one, square_two)


def solution(mesh):
    split = Mesh(mesh.devices.reshape(mesh.shape["head"], 8, 4, 2), ("head", *WIDE))
    placed = (
        P(WIDE, "head"),
        P(WIDE, "head"),
        P(WIDE, "head"),
        P(WIDE, "head"),
        P(None, WIDE, "head"),
        P(),
        P(),
        P(),
        P(),
        P(None, "head"),
        P(WIDE, "head", None, None),
        P(WIDE, "head", None, None),
        P(WIDE, None),
        P(WIDE, None),
        P(WIDE, None),
        P(WIDE, None),
        P(WIDE, None),
        P(WIDE, None),
    )
    return jax.shard_map(
        shards,
        mesh=split,
        in_specs=placed,
        out_specs=(
            P("head", WIDE),
            P(WIDE, None),
            P(WIDE, None),
            P(WIDE, None),
            P(WIDE, None),
            P(WIDE, None),
            P(WIDE, None),
        ),
        check_vma=False,
    )
```

```python
import math

import jax
import jax.numpy as jnp
from jax import lax
from jax.experimental import pallas as pl
from jax.experimental.pallas import tpu as pltpu
from jax.sharding import Mesh
from jax.sharding import PartitionSpec as P

HD = 128
REACH = 4
PROWS = 8
PCOLS = 8
PCH = 256
CMID = 128
CIN = 128
IMGTOK = 64
TOK = 256
WIDE = ("z", "yh", "yl")
LANES = 896

neg_big = -1e30
beta_one = 0.9
beta_two = 0.95
adam_eps = 1e-08
learn_rate = 0.02
decay_rate = 0.1
adam_step = 10
norm_eps = 1e-06
scale = 1.0 / math.sqrt(HD)

f32 = jnp.float32
bf16 = jnp.bfloat16


def nt(a, b):
    return lax.dot_general(a, b, (((1,), (1,)), ((), ())), preferred_element_type=f32)


def nn(a, b):
    return lax.dot_general(a, b, (((1,), (0,)), ((), ())), preferred_element_type=f32)


def tn(a, b):
    return lax.dot_general(a, b, (((0,), (0,)), ((), ())), preferred_element_type=f32)


def head_cols(h):
    return slice(h * HD, (h + 1) * HD)


def masked_scores(key_h, query_h, low, high, shift):
    scores = nt(key_h, query_h) * scale
    place = lax.broadcasted_iota(jnp.int32, scores.shape, 0) - shift
    seen = place >= low
    if high is not None:
        seen = seen & (place <= high)
    return jnp.where(seen, scores, neg_big)


def stats_kernel(meta, q, g, k0, v0, b1, b2, b3, b4, stats, scores_ref):
    near = [b1, b2, b3, b4]
    low = meta[1:2, :]
    high = meta[0:1, :]
    rows = []
    for h in range(2):
        cols = head_cols(h)
        query_h = q[:, cols]
        grad_h = g[:, cols]
        top = None
        for d in range(REACH + 1):
            key_h = k0[:, cols] if d == 0 else near[d - 1][0, :, cols]
            s = masked_scores(key_h, query_h, low, high if d == 0 else None, d * TOK)
            scores_ref[d] = s
            best = jnp.max(s, axis=0, keepdims=True)
            top = best if top is None else jnp.maximum(top, best)
        total = jnp.zeros((1, TOK), f32)
        for d in range(REACH + 1):
            e = jnp.exp(scores_ref[d] - top)
            scores_ref[d] = e
            total = total + jnp.sum(e, axis=0, keepdims=True)
        inverse = 1.0 / total
        delta = jnp.zeros((1, TOK), f32)
        for d in range(REACH + 1):
            value_h = v0[:, cols] if d == 0 else near[d - 1][1, :, cols]
            low_p = (scores_ref[d] * inverse).astype(bf16).astype(f32)
            delta = delta + jnp.sum(low_p * nt(value_h, grad_h), axis=0, keepdims=True)
        rows.append((top, inverse, delta))
    for h in range(2):
        for n in range(3):
            stats[3 * h + n : 3 * h + n + 1, :] = rows[h][n]
    stats[6:8, :] = jnp.zeros((2, TOK), f32)


def own_kernel(meta, stats, q, g, k0, v0, b1, b2, b3, b4, dq, dk, dv):
    near = [b1, b2, b3, b4]
    low = meta[1:2, :]
    high = meta[0:1, :]
    for h in range(2):
        cols = head_cols(h)
        query_h = q[:, cols]
        grad_h = g[:, cols]
        top = stats[3 * h : 3 * h + 1, :]
        inverse = stats[3 * h + 1 : 3 * h + 2, :]
        delta = stats[3 * h + 2 : 3 * h + 3, :]
        acc = jnp.zeros((TOK, HD), f32)
        for d in range(REACH + 1):
            key_h = k0[:, cols] if d == 0 else near[d - 1][0, :, cols]
            value_h = v0[:, cols] if d == 0 else near[d - 1][1, :, cols]
            s = masked_scores(key_h, query_h, low, high if d == 0 else None, d * TOK)
            prob = jnp.exp(s - top) * inverse
            ds = (prob * (nt(value_h, grad_h) - delta)).astype(bf16)
            acc = acc + tn(ds, key_h)
            if d == 0:
                dk[:, cols] = nn(ds, query_h)
                dv[:, cols] = nn(prob.astype(bf16), grad_h)
        dq[:, cols] = (acc * scale).astype(bf16)


def later_kernel(
    start, meta, k0, v0, a1, a2, a3, a4, s1, s2, s3, s4, dq, dk, dv, out, image
):
    later = [a1, a2, a3, a4]
    stats = [s1, s2, s3, s4]
    for h in range(2):
        cols = head_cols(h)
        key_h = k0[:, cols]
        value_h = v0[:, cols]
        dkey = dk[:, cols]
        dvalue = dv[:, cols]
        for d in range(1, REACH + 1):
            query_h = later[d - 1][0, :, cols]
            grad_h = later[d - 1][1, :, cols]
            row = stats[d - 1]
            low = meta[1 + d : 2 + d, :]
            s = masked_scores(key_h, query_h, low, None, 0)
            prob = jnp.exp(s - row[3 * h : 3 * h + 1, :]) * row[3 * h + 1 : 3 * h + 2, :]
            ds = (prob * (nt(value_h, grad_h) - row[3 * h + 2 : 3 * h + 3, :])).astype(bf16)
            dkey = dkey + nn(ds, query_h)
            dvalue = dvalue + nn(prob.astype(bf16), grad_h)
        out[1, :, cols] = (dkey * scale).astype(bf16)
        out[2, :, cols] = dvalue.astype(bf16)
    out[0] = dq[...]
    at = start[0]
    row = lax.broadcasted_iota(jnp.int32, (IMGTOK, TOK), 0) + at
    col = lax.broadcasted_iota(jnp.int32, (IMGTOK, TOK), 1)
    pick = jnp.where(row == col, 1.0, 0.0).astype(bf16)
    for n in range(3):
        image[n] = nn(pick, out[n]).astype(bf16)


def patch_kernel(w, g0, g1, pw, out, acc):
    step = pl.program_id(0)

    @pl.when(step == 0)
    def _():
        acc[...] = jnp.zeros_like(acc)

    t = jnp.zeros((2 * IMGTOK, TOK), f32)
    for p in range(3):
        both = jnp.concatenate([g0[p], g1[p]], axis=0)
        t = t + nt(both, w[0, :, p].reshape(TOK, TOK))
    acc[...] = acc[...] + nt(t.astype(bf16), pw[0])

    @pl.when(step == pl.num_programs(0) - 1)
    def _():
        out[...] = acc[...].astype(bf16)


def grad_kernel(w, g0, g1, out):
    for n, g in enumerate((g0, g1)):
        t = jnp.zeros((TOK, TOK), f32)
        for p in range(3):
            t = t + nt(w[0, :, p].reshape(TOK, TOK), g[p])
        out[0, :, n * TOK : (n + 1) * TOK] = t.astype(bf16)


def conv_kernel(scalars, pieces, k2, slope, left, out):
    head = scalars[0]
    present = scalars[1].astype(f32)
    total = jnp.zeros((IMGTOK, PCH), f32)
    for n in range(pieces.shape[0]):
        total = total + pieces[n].astype(f32)
    incoming = (total * present).astype(bf16)
    q = lax.broadcasted_iota(jnp.int32, (IMGTOK, IMGTOK), 0)
    p = lax.broadcasted_iota(jnp.int32, (IMGTOK, IMGTOK), 1)
    shifts = []
    for o in range(9):
        dr, dc = o // 3 - 1, o % 3 - 1
        hit = ((p >> 3) == (q >> 3) - dr) & ((p & 7) == (q & 7) - dc)
        shifts.append(jnp.where(hit, 1.0, 0.0).astype(bf16))
    dact = jnp.zeros((IMGTOK, 16), f32)
    for o in range(9):
        dact = dact + nt(nn(shifts[o], incoming).astype(bf16), k2[o])
    dpre = (dact * slope[...]).astype(bf16)
    ch = lax.broadcasted_iota(jnp.int32, (PCH, LANES), 0)
    lane = lax.broadcasted_iota(jnp.int32, (PCH, LANES), 1)
    spread = jnp.where((lane < 576) & ((lane & 31) == ch - 32 * head), 1.0, 0.0).astype(bf16)
    ch = lax.broadcasted_iota(jnp.int32, (16, LANES), 0)
    lane = lax.broadcasted_iota(jnp.int32, (16, LANES), 1)
    spread_first = jnp.where((lane >= 576) & ((lane & 15) == ch), 1.0, 0.0).astype(bf16)
    both = (nn(incoming, spread) + nn(dpre, spread_first)).astype(bf16)
    lane = lax.broadcasted_iota(jnp.int32, (IMGTOK, LANES), 1)
    second = jnp.where(lane >= 288, lane - 288, lane) >> 5
    first = (jnp.where(lane >= 720, lane - 720, lane - 576)) >> 4
    which = jnp.where(lane < 576, second, first)
    moved = jnp.zeros((IMGTOK, LANES), f32)
    zero = jnp.zeros((IMGTOK, LANES), bf16)
    for o in range(9):
        moved = moved + nn(shifts[o], jnp.where(which == o, both, zero))
    moved = moved.astype(bf16)
    ends = (0, 288, 576, 720, 864)
    result = jnp.zeros((IMGTOK, LANES), f32)
    for n in range(4):
        part = jnp.where((lane >= ends[n]) & (lane < ends[n + 1]), moved, zero)
        result = result + nn(left[n], part)
    out[...] = result.astype(bf16)


def whole(space=None):
    return pl.BlockSpec(memory_space=pltpu.VMEM if space is None else space)


def on_chip(kernel, shapes, count, scratch=(), scalars=0):
    return pl.pallas_call(
        kernel,
        out_shape=shapes,
        in_specs=[whole(pltpu.SMEM)] * scalars + [whole()] * (count - scalars),
        out_specs=jax.tree.map(lambda _: whole(), shapes),
        scratch_shapes=list(scratch),
    )


def spec_of(shape, dtype):
    return jax.ShapeDtypeStruct(shape, dtype)


def pick_entry(lookup, wanted):
    return jnp.sum(jnp.where(jnp.arange(lookup.shape[0]) == wanted, lookup, 0))


def passed_along(block, axis, distance):
    devices = range(lax.axis_size(axis))
    route = [(i - distance, i) for i in devices if i - distance in devices]
    return lax.ppermute(block, axis, route)


def ringed(value, axis, distance):
    count = lax.axis_size(axis)
    return lax.ppermute(value, axis, [(i, (i + distance) % count) for i in range(count)])


def swapped(value):
    return lax.ppermute(value, "yl", [(0, 1), (1, 0)])


def exchanged(pieces, axis):
    return lax.all_to_all(pieces, axis, split_axis=0, concat_axis=0, tiled=True)


def sent_to_all(value, axis):
    return exchanged(jnp.broadcast_to(value, (lax.axis_size(axis), *value.shape)), axis)


def adam_update(param, mean, square, grad):
    new_mean = beta_one * mean + (1.0 - beta_one) * grad
    new_square = beta_two * square + (1.0 - beta_two) * grad * grad
    fixed_mean = new_mean / (1.0 - beta_one**adam_step)
    fixed_square = new_square / (1.0 - beta_two**adam_step)
    new_param = param - learn_rate * (
        fixed_mean / (jnp.sqrt(fixed_square) + adam_eps) + decay_rate * param
    )
    return (new_param, new_mean, new_square)


def seen_range(block, doc_lengths, image_count, image_offset):
    index = jnp.arange(doc_lengths.shape[0])
    ends = jnp.sum(jnp.where(index[None, :] <= index[:, None], doc_lengths[None, :], 0), axis=1)
    starts = ends - doc_lengths
    base = block * TOK
    places = base + jnp.arange((REACH + 1) * TOK, dtype=jnp.int32)
    begun = starts[:, None] <= places[None, :]
    low = jnp.max(jnp.where(begun, starts[:, None], 0), axis=0)
    own = places[:TOK]
    over = ends[:, None] > own[None, :]
    doc_end = jnp.min(jnp.where(over, ends[:, None], jnp.int32(1 << 30)), axis=0)
    present = pick_entry(image_count, block)
    offset = pick_entry(image_offset, block)
    local = own - base
    inside = (present > 0) & (local >= offset) & (local < offset + IMGTOK)
    high = jnp.where(
        inside, jnp.maximum(own, jnp.minimum(base + offset + IMGTOK, doc_end) - 1), own
    )
    rows = [high[None], low.reshape(REACH + 1, TOK), jnp.zeros((2, TOK), jnp.int32) + base]
    return jnp.concatenate(rows, axis=0) - base, present, offset


def shards(
    queries,
    keys,
    values,
    out_grad,
    qkv_weight,
    doc_lengths,
    image_count,
    image_offset,
    slab_owner,
    patch_weight,
    conv_input,
    pre_act,
    kernel_first,
    kernel_second,
    mean_first,
    mean_second,
    square_first,
    square_second,
):
    device_index = lax.axis_index(WIDE)
    head_index = lax.axis_index("head")
    side = lax.axis_index("yl")

    before = jnp.stack([keys, values])
    after = jnp.stack([queries, out_grad])
    earlier, later = [], []
    for _ in range(REACH):
        before = passed_along(before, WIDE, 1)
        after = passed_along(after, WIDE, -1)
        earlier.append(before)
        later.append(after)

    meta, present, offset = seen_range(device_index, doc_lengths, image_count, image_offset)

    place_z = lax.axis_index("z")
    quad = sent_to_all(qkv_weight, "yh")
    weights = jnp.zeros((8, *quad.shape), quad.dtype)
    weights = lax.dynamic_update_index_in_dim(weights, quad, place_z, 0)
    up = down = quad
    for k in range(1, 5):
        up = ringed(up, "z", 1)
        weights = lax.dynamic_update_index_in_dim(weights, up, (place_z - k) % 8, 0)
        if k < 4:
            down = ringed(down, "z", -1)
            weights = lax.dynamic_update_index_in_dim(weights, down, (place_z + k) % 8, 0)

    half_patch = lax.dynamic_index_in_dim(
        patch_weight.reshape(PCH, 4, 2, 64), side, 2, keepdims=False
    ).reshape(PCH, TOK)
    patch_half = sent_to_all(half_patch, "head")
    rows = jnp.concatenate([conv_input.reshape(PCOLS, CIN), pre_act.reshape(PCOLS, CMID)], axis=1)
    slots = sent_to_all(rows, WIDE)
    slot = pick_entry(slab_owner, device_index)
    my_rows = lax.dynamic_index_in_dim(slots, slot, 0, keepdims=False)
    picture = sent_to_all(my_rows, "head").reshape(IMGTOK, CIN + CMID)
    turned = [(a * 8 + b, b * 8 + a) for a in range(8) for b in range(8)]
    kernel_rows = lax.ppermute(kernel_second.astype(bf16), ("head", "z"), turned)
    kernel_mine = sent_to_all(kernel_rows, ("yh", "yl")).reshape(16, 9, PCH).transpose(1, 0, 2)

    conv_img = picture[:, :CIN]
    pre_img = picture[:, CIN:].astype(f32)
    act = jax.nn.silu(pre_img).astype(bf16)
    left = jnp.concatenate([act.T.reshape(64, 2, 64), conv_img.T.reshape(64, 2, 64)], axis=1)
    left = left.transpose(1, 0, 2)
    sig = jax.nn.sigmoid(pre_img)
    slope = sig * (1.0 + pre_img * (1.0 - sig))
    slope = lax.dynamic_slice_in_dim(slope, head_index * 16, 16, 1)

    stats = on_chip(
        stats_kernel,
        spec_of((8, TOK), f32),
        9,
        [pltpu.VMEM((REACH + 1, TOK, TOK), f32)],
    )(meta, queries, out_grad, keys, values, *earlier)
    stats_later = [passed_along(stats, WIDE, -d) for d in range(1, REACH + 1)]
    dq, dk, dv = on_chip(
        own_kernel,
        (spec_of((TOK, TOK), bf16), spec_of((TOK, TOK), f32), spec_of((TOK, TOK), f32)),
        10,
    )(meta, stats, queries, out_grad, keys, values, *earlier)
    grads, image_grads = on_chip(
        later_kernel,
        (spec_of((3, TOK, TOK), bf16), spec_of((3, IMGTOK, TOK), bf16)),
        15,
        scalars=1,
    )(offset[None], meta, keys, values, *later, *stats_later, dq, dk, dv)

    image_other = swapped(image_grads)
    grads_other = swapped(grads)

    def in_order(own, other):
        return jnp.where(side == 0, own, other), jnp.where(side == 0, other, own)

    weight_block = pl.BlockSpec((1, 4, 3, 64, TOK), lambda i: (i, 0, 0, 0, 0))

    def fixed(*shape):
        return pl.BlockSpec(shape, lambda i: (0,) * len(shape))

    patch_part = pl.pallas_call(
        patch_kernel,
        out_shape=spec_of((2 * IMGTOK, PCH), bf16),
        grid=(8,),
        in_specs=[
            weight_block,
            fixed(3, IMGTOK, TOK),
            fixed(3, IMGTOK, TOK),
            pl.BlockSpec((1, PCH, TOK), lambda i: (i, 0, 0)),
        ],
        out_specs=fixed(2 * IMGTOK, PCH),
        scratch_shapes=[pltpu.VMEM((2 * IMGTOK, PCH), f32)],
    )(weights, *in_order(image_grads, image_other), patch_half)
    pieces = exchanged(
        jnp.broadcast_to(patch_part[None], (8, 2 * IMGTOK, PCH)).reshape(16, IMGTOK, PCH), ("head", "yl")
    )

    halves = pl.pallas_call(
        grad_kernel,
        out_shape=spec_of((8, TOK, 2 * TOK), bf16),
        grid=(8,),
        in_specs=[weight_block, fixed(3, TOK, TOK), fixed(3, TOK, TOK)],
        out_specs=pl.BlockSpec((1, TOK, 2 * TOK), lambda i: (i, 0, 0)),
    )(weights, *in_order(grads, grads_other))
    pieces, halves = lax.optimization_barrier((pieces, halves))
    traded = exchanged(halves, "head")

    flags = jnp.stack([head_index.astype(jnp.int32), present.astype(jnp.int32)])
    partial = on_chip(conv_kernel, spec_of((64, LANES), bf16), 5, scalars=1)(
        flags, pieces, kernel_mine, slope, left
    )

    owned = exchanged(partial.reshape(64, 7, 128), WIDE)
    owned = jnp.sum(owned.astype(f32), axis=0)
    squares = jnp.broadcast_to(jnp.sum(owned * owned), (1, 128))
    squares = jnp.sum(sent_to_all(squares, WIDE), axis=0)

    summed = jnp.sum(traded.astype(f32), axis=0).astype(bf16)
    summed, squares = lax.optimization_barrier((summed, squares))
    mine, theirs = in_order(summed[:, :TOK], summed[:, TOK:])
    arrived = swapped(theirs)
    even, odd = in_order(mine, arrived)
    input_grad_t = jnp.stack([even.reshape(4, 64, TOK), odd.reshape(4, 64, TOK)], axis=1)
    input_grad_t = input_grad_t.reshape(512, TOK)

    together = sent_to_all(jnp.concatenate([owned, squares], axis=0), "head")
    total = jnp.sum(together[:, 7, 0])
    columns = together[:, :7].reshape(8, LANES)
    grad_second = (
        columns[:, :576].reshape(8, 2, 9, 32).transpose(1, 2, 0, 3).reshape(18, PCH)
    )
    grad_first = (
        columns[:, 576:864].reshape(8, 2, 9, 16).transpose(1, 2, 0, 3).reshape(18, CMID)
    )
    limit = 0.5 * math.sqrt(9 * CIN * CMID + 9 * CMID * PCH)
    factor = jnp.minimum(1.0, limit / (jnp.sqrt(total) + norm_eps))
    kernel_one, mean_one, square_one = adam_update(
        kernel_first, mean_first, square_first, grad_first * factor
    )
    kernel_two, mean_two, square_two = adam_update(
        kernel_second, mean_second, square_second, grad_second * factor
    )
    return (input_grad_t, kernel_one, kernel_two, mean_one, mean_two, square_one, square_two)


def solution(mesh):
    split = Mesh(mesh.devices.reshape(mesh.shape["head"], 8, 4, 2), ("head", *WIDE))
    placed = (
        P(WIDE, "head"),
        P(WIDE, "head"),
        P(WIDE, "head"),
        P(WIDE, "head"),
        P(None, WIDE, "head"),
        P(),
        P(),
        P(),
        P(),
        P(None, "head"),
        P(WIDE, "head", None, None),
        P(WIDE, "head", None, None),
        P(WIDE, None),
        P(WIDE, None),
        P(WIDE, None),
        P(WIDE, None),
        P(WIDE, None),
        P(WIDE, None),
    )
    return jax.shard_map(
        shards,
        mesh=split,
        in_specs=placed,
        out_specs=(
            P("head", WIDE),
            P(WIDE, None),
            P(WIDE, None),
            P(WIDE, None),
            P(WIDE, None),
            P(WIDE, None),
            P(WIDE, None),
        ),
        check_vma=False,
    )
```

```python
import math

import jax
import jax.numpy as jnp
from jax import lax
from jax.experimental import pallas as pl
from jax.experimental.pallas import tpu as pltpu
from jax.sharding import Mesh
from jax.sharding import PartitionSpec as P

HD = 128
REACH = 4
PROWS = 8
PCOLS = 8
PCH = 256
CMID = 128
CIN = 128
IMGTOK = 64
TOK = 256
TALL = ("yh", "yl")
WIDE = ("z", *TALL)
LANES = 896

neg_big = -1e30
beta_one = 0.9
beta_two = 0.95
adam_eps = 1e-08
learn_rate = 0.02
decay_rate = 0.1
adam_step = 10
norm_eps = 1e-06
scale = 1.0 / math.sqrt(HD)

f32 = jnp.float32
bf16 = jnp.bfloat16


def nt(a, b):
    return lax.dot_general(a, b, (((1,), (1,)), ((), ())), preferred_element_type=f32)


def nn(a, b):
    return lax.dot_general(a, b, (((1,), (0,)), ((), ())), preferred_element_type=f32)


def tn(a, b):
    return lax.dot_general(a, b, (((0,), (0,)), ((), ())), preferred_element_type=f32)


def head_cols(h):
    return slice(h * HD, (h + 1) * HD)


def masked_scores(key_h, query_h, low, high, shift):
    scores = nt(key_h, query_h) * scale
    place = lax.broadcasted_iota(jnp.int32, scores.shape, 0) - shift
    seen = place >= low
    if high is not None:
        seen = seen & (place <= high)
    return jnp.where(seen, scores, neg_big)


def stats_kernel(meta, q, g, k0, v0, b1, b2, b3, b4, stats, scores_ref):
    near = [b1, b2, b3, b4]
    low = meta[1:2, :]
    high = meta[0:1, :]
    rows = []
    for h in range(2):
        cols = head_cols(h)
        query_h = q[:, cols]
        grad_h = g[:, cols]
        top = None
        for d in range(REACH + 1):
            key_h = k0[:, cols] if d == 0 else near[d - 1][0, :, cols]
            s = masked_scores(key_h, query_h, low, high if d == 0 else None, d * TOK)
            scores_ref[d] = s
            best = jnp.max(s, axis=0, keepdims=True)
            top = best if top is None else jnp.maximum(top, best)
        total = jnp.zeros((1, TOK), f32)
        for d in range(REACH + 1):
            e = jnp.exp(scores_ref[d] - top)
            scores_ref[d] = e
            total = total + jnp.sum(e, axis=0, keepdims=True)
        inverse = 1.0 / total
        delta = jnp.zeros((1, TOK), f32)
        for d in range(REACH + 1):
            value_h = v0[:, cols] if d == 0 else near[d - 1][1, :, cols]
            low_p = (scores_ref[d] * inverse).astype(bf16).astype(f32)
            delta = delta + jnp.sum(low_p * nt(value_h, grad_h), axis=0, keepdims=True)
        rows.append((top, inverse, delta))
    for h in range(2):
        for n in range(3):
            stats[3 * h + n : 3 * h + n + 1, :] = rows[h][n]
    stats[6:8, :] = jnp.zeros((2, TOK), f32)


def own_kernel(meta, stats, q, g, k0, v0, b1, b2, b3, b4, dq, dk, dv):
    near = [b1, b2, b3, b4]
    low = meta[1:2, :]
    high = meta[0:1, :]
    for h in range(2):
        cols = head_cols(h)
        query_h = q[:, cols]
        grad_h = g[:, cols]
        top = stats[3 * h : 3 * h + 1, :]
        inverse = stats[3 * h + 1 : 3 * h + 2, :]
        delta = stats[3 * h + 2 : 3 * h + 3, :]
        acc = jnp.zeros((TOK, HD), f32)
        for d in range(REACH + 1):
            key_h = k0[:, cols] if d == 0 else near[d - 1][0, :, cols]
            value_h = v0[:, cols] if d == 0 else near[d - 1][1, :, cols]
            s = masked_scores(key_h, query_h, low, high if d == 0 else None, d * TOK)
            prob = jnp.exp(s - top) * inverse
            ds = (prob * (nt(value_h, grad_h) - delta)).astype(bf16)
            acc = acc + tn(ds, key_h)
            if d == 0:
                dk[:, cols] = nn(ds, query_h)
                dv[:, cols] = nn(prob.astype(bf16), grad_h)
        dq[:, cols] = (acc * scale).astype(bf16)


def later_kernel(
    start, meta, k0, v0, a1, a2, a3, a4, s1, s2, s3, s4, dq, dk, dv, out, image
):
    later = [a1, a2, a3, a4]
    stats = [s1, s2, s3, s4]
    for h in range(2):
        cols = head_cols(h)
        key_h = k0[:, cols]
        value_h = v0[:, cols]
        dkey = dk[:, cols]
        dvalue = dv[:, cols]
        for d in range(1, REACH + 1):
            query_h = later[d - 1][0, :, cols]
            grad_h = later[d - 1][1, :, cols]
            row = stats[d - 1]
            low = meta[1 + d : 2 + d, :]
            s = masked_scores(key_h, query_h, low, None, 0)
            prob = jnp.exp(s - row[3 * h : 3 * h + 1, :]) * row[3 * h + 1 : 3 * h + 2, :]
            ds = (prob * (nt(value_h, grad_h) - row[3 * h + 2 : 3 * h + 3, :])).astype(bf16)
            dkey = dkey + nn(ds, query_h)
            dvalue = dvalue + nn(prob.astype(bf16), grad_h)
        out[1, :, cols] = (dkey * scale).astype(bf16)
        out[2, :, cols] = dvalue.astype(bf16)
    out[0] = dq[...]
    at = start[0]
    row = lax.broadcasted_iota(jnp.int32, (IMGTOK, TOK), 0) + at
    col = lax.broadcasted_iota(jnp.int32, (IMGTOK, TOK), 1)
    pick = jnp.where(row == col, 1.0, 0.0).astype(bf16)
    for n in range(3):
        image[n] = nn(pick, out[n]).astype(bf16)


def paired(flags, own, other):
    first = flags[0] == 0
    return jnp.where(first, own, other), jnp.where(first, other, own)


def patch_kernel(flags, w, own, other, pw, out, acc):
    step = pl.program_id(0)

    @pl.when(step == 0)
    def _():
        acc[...] = jnp.zeros_like(acc)

    for n in range(2):
        t = jnp.zeros((2 * IMGTOK, TOK), f32)
        for p in range(3):
            both = jnp.concatenate(paired(flags, own[p], other[p]), axis=0)
            t = t + nt(both, w[n, :, p].reshape(TOK, TOK))
        acc[...] = acc[...] + nt(t.astype(bf16), pw[n, :PCH])

    @pl.when(step == pl.num_programs(0) - 1)
    def _():
        total = acc[...].astype(bf16)
        for n in range(8):
            out[n] = total


def grad_kernel(flags, w, own, other, mine, theirs):
    core = flags[1]
    for m, out in ((core, mine), (1 - core, theirs)):
        for n in range(2):
            t = jnp.zeros((TOK, TOK), f32)
            for p in range(3):
                t = t + nt(w[m, :, p].reshape(TOK, TOK), paired(flags, own[p], other[p])[n])
            out[0, :, n * TOK : (n + 1) * TOK] = t.astype(bf16)


def conv_kernel(scalars, pieces, k2, slope, left, out):
    head = scalars[0]
    present = scalars[1].astype(f32)
    total = jnp.zeros((IMGTOK, PCH), f32)
    for n in range(pieces.shape[0]):
        total = total + pieces[n].astype(f32)
    incoming = (total * present).astype(bf16)
    q = lax.broadcasted_iota(jnp.int32, (IMGTOK, IMGTOK), 0)
    p = lax.broadcasted_iota(jnp.int32, (IMGTOK, IMGTOK), 1)
    shifts = []
    for o in range(9):
        dr, dc = o // 3 - 1, o % 3 - 1
        hit = ((p >> 3) == (q >> 3) - dr) & ((p & 7) == (q & 7) - dc)
        shifts.append(jnp.where(hit, 1.0, 0.0).astype(bf16))
    dact = jnp.zeros((IMGTOK, 16), f32)
    for o in range(9):
        dact = dact + nt(nn(shifts[o], incoming).astype(bf16), k2[o])
    dpre = (dact * slope[...]).astype(bf16)
    ch = lax.broadcasted_iota(jnp.int32, (PCH, LANES), 0)
    lane = lax.broadcasted_iota(jnp.int32, (PCH, LANES), 1)
    spread = jnp.where((lane < 576) & ((lane & 31) == ch - 32 * head), 1.0, 0.0).astype(bf16)
    ch = lax.broadcasted_iota(jnp.int32, (16, LANES), 0)
    lane = lax.broadcasted_iota(jnp.int32, (16, LANES), 1)
    spread_first = jnp.where((lane >= 576) & ((lane & 15) == ch), 1.0, 0.0).astype(bf16)
    both = (nn(incoming, spread) + nn(dpre, spread_first)).astype(bf16)
    lane = lax.broadcasted_iota(jnp.int32, (IMGTOK, LANES), 1)
    second = jnp.where(lane >= 288, lane - 288, lane) >> 5
    first = (jnp.where(lane >= 720, lane - 720, lane - 576)) >> 4
    which = jnp.where(lane < 576, second, first)
    moved = jnp.zeros((IMGTOK, LANES), f32)
    zero = jnp.zeros((IMGTOK, LANES), bf16)
    for o in range(9):
        moved = moved + nn(shifts[o], jnp.where(which == o, both, zero))
    moved = moved.astype(bf16)
    ends = (0, 288, 576, 720, 864)
    result = jnp.zeros((IMGTOK, LANES), f32)
    for n in range(4):
        part = jnp.where((lane >= ends[n]) & (lane < ends[n + 1]), moved, zero)
        result = result + nn(left[n], part)
    for n in range(7):
        out[:, n, :] = result[:, n * 128 : (n + 1) * 128].astype(bf16)


def whole(space=None):
    return pl.BlockSpec(memory_space=pltpu.VMEM if space is None else space)


def on_chip(kernel, shapes, count, scratch=(), scalars=0):
    return pl.pallas_call(
        kernel,
        out_shape=shapes,
        in_specs=[whole(pltpu.SMEM)] * scalars + [whole()] * (count - scalars),
        out_specs=jax.tree.map(lambda _: whole(), shapes),
        scratch_shapes=list(scratch),
    )


def spec_of(shape, dtype):
    return jax.ShapeDtypeStruct(shape, dtype)


def pick_entry(lookup, wanted):
    return jnp.sum(jnp.where(jnp.arange(lookup.shape[0]) == wanted, lookup, 0))


def passed_along(block, axis, distance):
    devices = range(lax.axis_size(axis))
    route = [(i - distance, i) for i in devices if i - distance in devices]
    return lax.ppermute(block, axis, route)


def swapped(value):
    return lax.ppermute(value, "yl", [(0, 1), (1, 0)])


def once_here(value, reached):
    return lax.optimization_barrier((value, reached))[0]


def exchanged(pieces, axis):
    return lax.all_to_all(pieces, axis, split_axis=0, concat_axis=0, tiled=True)


def sent_to_all(value, axis):
    return exchanged(jnp.broadcast_to(value, (lax.axis_size(axis), *value.shape)), axis)


def summed_low(pieces):
    return jnp.sum(pieces.astype(f32), axis=0).astype(bf16)


def adam_update(param, mean, square, grad):
    new_mean = beta_one * mean + (1.0 - beta_one) * grad
    new_square = beta_two * square + (1.0 - beta_two) * grad * grad
    fixed_mean = new_mean / (1.0 - beta_one**adam_step)
    fixed_square = new_square / (1.0 - beta_two**adam_step)
    new_param = param - learn_rate * (
        fixed_mean / (jnp.sqrt(fixed_square) + adam_eps) + decay_rate * param
    )
    return (new_param, new_mean, new_square)


def seen_range(block, doc_lengths, image_count, image_offset):
    index = jnp.arange(doc_lengths.shape[0])
    ends = jnp.sum(jnp.where(index[None, :] <= index[:, None], doc_lengths[None, :], 0), axis=1)
    starts = ends - doc_lengths
    base = block * TOK
    places = base + jnp.arange((REACH + 1) * TOK, dtype=jnp.int32)
    begun = starts[:, None] <= places[None, :]
    low = jnp.max(jnp.where(begun, starts[:, None], 0), axis=0)
    own = places[:TOK]
    over = ends[:, None] > own[None, :]
    doc_end = jnp.min(jnp.where(over, ends[:, None], jnp.int32(1 << 30)), axis=0)
    present = pick_entry(image_count, block)
    offset = pick_entry(image_offset, block)
    local = own - base
    inside = (present > 0) & (local >= offset) & (local < offset + IMGTOK)
    high = jnp.where(
        inside, jnp.maximum(own, jnp.minimum(base + offset + IMGTOK, doc_end) - 1), own
    )
    rows = [high[None], low.reshape(REACH + 1, TOK), jnp.zeros((2, TOK), jnp.int32) + base]
    return jnp.concatenate(rows, axis=0) - base, present, offset


def shards(
    queries,
    keys,
    values,
    out_grad,
    qkv_weight,
    doc_lengths,
    image_count,
    image_offset,
    slab_owner,
    patch_weight,
    conv_input,
    pre_act,
    kernel_first,
    kernel_second,
    mean_first,
    mean_second,
    square_first,
    square_second,
):
    device_index = lax.axis_index(WIDE)
    head_index = lax.axis_index("head")
    side = lax.axis_index("yl")

    before = jnp.stack([keys, values])
    after = jnp.stack([queries, out_grad])
    earlier, later = [], []
    meta, present, offset = seen_range(device_index, doc_lengths, image_count, image_offset)
    for hop in range(REACH):
        before = passed_along(before, WIDE, 1)
        after = passed_along(after, WIDE, -1)
        if hop == REACH - 2:
            before, after, meta = lax.optimization_barrier((before, after, meta))
        else:
            before, after = lax.optimization_barrier((before, after))
        earlier.append(before)
        later.append(after)

    stats = on_chip(
        stats_kernel,
        spec_of((8, TOK), f32),
        9,
        [pltpu.VMEM((REACH + 1, TOK, TOK), f32)],
    )(meta, queries, out_grad, keys, values, *earlier)

    quad = once_here(sent_to_all(qkv_weight, "yh"), earlier[0])
    weights = lax.all_gather(quad, "z", axis=0)
    slot_rows = jnp.concatenate(
        [conv_input.reshape(PCOLS, CIN), pre_act.reshape(PCOLS, CMID)], axis=1
    )
    slot_rows = jnp.concatenate([slot_rows, kernel_second.astype(bf16)], axis=0)
    along_z = sent_to_all(once_here(slot_rows, earlier[1]), "z")
    kernel_rows = lax.dynamic_index_in_dim(along_z[:, PCOLS:], head_index, 0, keepdims=False)
    slot_rows = along_z[:, :PCOLS].reshape(64, PCH)
    along_y = jnp.concatenate([slot_rows, kernel_rows], axis=0)
    along_y = sent_to_all(once_here(along_y, earlier[2]), TALL)
    along_y = once_here(along_y, stats)
    kernel_mine = along_y[:, 64:].reshape(16, 9, PCH).transpose(1, 0, 2)
    slot = pick_entry(slab_owner, device_index)
    my_rows = along_y[:, :64].reshape(8, 8, PCOLS, PCH)
    my_rows = lax.dynamic_slice(
        my_rows, (slot % 8, slot // 8, 0, 0), (1, 1, PCOLS, PCH)
    ).reshape(PCOLS, PCH)
    half_patch = lax.dynamic_index_in_dim(
        patch_weight.reshape(PCH, 4, 2, 64), side, 2, keepdims=False
    ).reshape(PCH, TOK)
    along_head = sent_to_all(jnp.concatenate([half_patch, my_rows], axis=0), "head")
    picture = along_head[:, PCH:].reshape(IMGTOK, CIN + CMID)

    conv_img = picture[:, :CIN]
    pre_img = picture[:, CIN:].astype(f32)
    act = jax.nn.silu(pre_img).astype(bf16)
    left = jnp.concatenate([act.T.reshape(64, 2, 64), conv_img.T.reshape(64, 2, 64)], axis=1)
    left = left.transpose(1, 0, 2)
    sig = jax.nn.sigmoid(pre_img)
    slope = sig * (1.0 + pre_img * (1.0 - sig))
    slope = lax.dynamic_slice_in_dim(slope, head_index * 16, 16, 1)

    stats_later = [passed_along(stats, WIDE, -d) for d in range(1, REACH + 1)]
    dq, dk, dv = on_chip(
        own_kernel,
        (spec_of((TOK, TOK), bf16), spec_of((TOK, TOK), f32), spec_of((TOK, TOK), f32)),
        10,
    )(meta, stats, queries, out_grad, keys, values, *earlier)
    grads, image_grads = on_chip(
        later_kernel,
        (spec_of((3, TOK, TOK), bf16), spec_of((3, IMGTOK, TOK), bf16)),
        15,
        scalars=1,
    )(offset[None], meta, keys, values, *later, *stats_later, dq, dk, dv)

    image_other = swapped(image_grads)
    grads_other = swapped(once_here(grads, image_other))
    core = head_index % 2
    flags = jnp.stack([side.astype(jnp.int32), core.astype(jnp.int32)])

    def in_order(own, other):
        return jnp.where(side == 0, own, other), jnp.where(side == 0, other, own)

    weight_block = pl.BlockSpec((2, 4, 3, 64, TOK), lambda i: (i, 0, 0, 0, 0))
    out_block = pl.BlockSpec((1, TOK, 2 * TOK), lambda i: (i, 0, 0))

    def fixed(*shape):
        return pl.BlockSpec(shape, lambda i: (0,) * len(shape))

    pieces = pl.pallas_call(
        patch_kernel,
        out_shape=spec_of((8, 2 * IMGTOK, PCH), bf16),
        grid=(4,),
        in_specs=[
            whole(pltpu.SMEM),
            weight_block,
            fixed(3, IMGTOK, TOK),
            fixed(3, IMGTOK, TOK),
            pl.BlockSpec((2, PCH + PCOLS, TOK), lambda i: (i, 0, 0)),
        ],
        out_specs=fixed(8, 2 * IMGTOK, PCH),
        scratch_shapes=[pltpu.VMEM((2 * IMGTOK, PCH), f32)],
    )(flags, weights, image_grads, image_other, along_head)
    pieces = exchanged(pieces.reshape(16, IMGTOK, PCH), ("head", "yl"))

    mine, theirs = pl.pallas_call(
        grad_kernel,
        out_shape=[spec_of((4, TOK, 2 * TOK), bf16)] * 2,
        grid=(4,),
        in_specs=[
            whole(pltpu.SMEM),
            weight_block,
            fixed(3, TOK, TOK),
            fixed(3, TOK, TOK),
        ],
        out_specs=[out_block] * 2,
    )(flags, weights, grads, grads_other)
    pieces, theirs, left, slope, kernel_mine = lax.optimization_barrier(
        (pieces, theirs, left, slope, kernel_mine)
    )
    arrived = lax.ppermute(theirs, "head", [(i, i ^ 1) for i in range(8)])

    flags = jnp.stack([head_index.astype(jnp.int32), present.astype(jnp.int32)])
    partial = on_chip(conv_kernel, spec_of((64, 7, 128), bf16), 5, scalars=1)(
        flags, pieces, kernel_mine, slope, left
    )

    owned = exchanged(partial, WIDE)

    chip = (mine.astype(f32) + arrived.astype(f32)).astype(bf16)
    place_x = head_index // 2
    total = lax.dynamic_index_in_dim(chip, place_x, 0, keepdims=False).astype(f32)
    slices = [
        lax.dynamic_index_in_dim(chip, (place_x + d) % 4, 0, keepdims=False) for d in range(1, 4)
    ]
    owned = jnp.sum(once_here(owned, slices).astype(f32), axis=0)
    for d, piece in zip(range(1, 4), slices):
        piece = lax.ppermute(piece, "head", [(i, (i + 2 * d) % 8) for i in range(8)])
        total = total + piece.astype(f32)

    squares = jnp.broadcast_to(jnp.sum(owned * owned), (1, 128))
    squares = jnp.sum(sent_to_all(squares, WIDE), axis=0)
    summed = total.astype(bf16)
    summed, squares = lax.optimization_barrier((summed, squares))
    mine, theirs = in_order(summed[:, :TOK], summed[:, TOK:])
    even, odd = in_order(mine, swapped(theirs))
    input_grad_t = jnp.stack([even.reshape(4, 64, TOK), odd.reshape(4, 64, TOK)], axis=1)
    input_grad_t = input_grad_t.reshape(512, TOK)

    together = sent_to_all(jnp.concatenate([owned, squares], axis=0), "head")
    total = jnp.sum(together[:, 7, 0])
    columns = together[:, :7].reshape(8, LANES)
    grad_second = (
        columns[:, :576].reshape(8, 2, 9, 32).transpose(1, 2, 0, 3).reshape(18, PCH)
    )
    grad_first = (
        columns[:, 576:864].reshape(8, 2, 9, 16).transpose(1, 2, 0, 3).reshape(18, CMID)
    )
    limit = 0.5 * math.sqrt(9 * CIN * CMID + 9 * CMID * PCH)
    factor = jnp.minimum(1.0, limit / (jnp.sqrt(total) + norm_eps))
    kernel_one, mean_one, square_one = adam_update(
        kernel_first, mean_first, square_first, grad_first * factor
    )
    kernel_two, mean_two, square_two = adam_update(
        kernel_second, mean_second, square_second, grad_second * factor
    )
    return (input_grad_t, kernel_one, kernel_two, mean_one, mean_two, square_one, square_two)


def solution(mesh):
    split = Mesh(mesh.devices.reshape(mesh.shape["head"], 8, 4, 2), ("head", *WIDE))
    placed = (
        P(WIDE, "head"),
        P(WIDE, "head"),
        P(WIDE, "head"),
        P(WIDE, "head"),
        P(None, WIDE, "head"),
        P(),
        P(),
        P(),
        P(),
        P(None, "head"),
        P(WIDE, "head", None, None),
        P(WIDE, "head", None, None),
        P(WIDE, None),
        P(WIDE, None),
        P(WIDE, None),
        P(WIDE, None),
        P(WIDE, None),
        P(WIDE, None),
    )
    return jax.shard_map(
        shards,
        mesh=split,
        in_specs=placed,
        out_specs=(
            P("head", WIDE),
            P(WIDE, None),
            P(WIDE, None),
            P(WIDE, None),
            P(WIDE, None),
            P(WIDE, None),
            P(WIDE, None),
        ),
        check_vma=False,
    )
```

```python
import math

import jax
import jax.numpy as jnp
from jax import lax
from jax.experimental import pallas as pl
from jax.experimental.pallas import tpu as pltpu
from jax.sharding import Mesh
from jax.sharding import PartitionSpec as P


HD = 128
REACH = 4
PCOLS = 8
PCH = 256
CMID = 128
CIN = 128
IMGTOK = 64
TOK = 256
TALL = ("yh", "yl")
WIDE = ("z", *TALL)
LANES = 896

neg_big = -1e30
beta_one = 0.9
beta_two = 0.95
adam_eps = 1e-08
learn_rate = 0.02
decay_rate = 0.1
adam_step = 10
norm_eps = 1e-06
scale = 1.0 / math.sqrt(HD)

f32 = jnp.float32
bf16 = jnp.bfloat16


def nt(a, b):
    return lax.dot_general(a, b, (((1,), (1,)), ((), ())), preferred_element_type=f32)


def nn(a, b):
    return lax.dot_general(a, b, (((1,), (0,)), ((), ())), preferred_element_type=f32)


def tn(a, b):
    return lax.dot_general(a, b, (((0,), (0,)), ((), ())), preferred_element_type=f32)


def head_cols(h):
    return slice(h * HD, (h + 1) * HD)


def masked_scores(key_h, query_h, low, high, shift):
    scores = nt(key_h, query_h) * scale
    place = lax.broadcasted_iota(jnp.int32, scores.shape, 0) - shift
    seen = place >= low
    if high is not None:
        seen = seen & (place <= high)
    return jnp.where(seen, scores, neg_big)


def stats_kernel(meta, q, g, k0, v0, b1, b2, b3, b4, stats, scores_ref):
    near = [b1, b2, b3, b4]
    low = meta[1:2, :]
    high = meta[0:1, :]
    rows = []
    for h in range(2):
        cols = head_cols(h)
        query_h = q[:, cols]
        grad_h = g[:, cols]
        top = None
        for d in range(REACH + 1):
            key_h = k0[:, cols] if d == 0 else near[d - 1][0, :, cols]
            s = masked_scores(key_h, query_h, low, high if d == 0 else None, d * TOK)
            scores_ref[d] = s
            best = jnp.max(s, axis=0, keepdims=True)
            top = best if top is None else jnp.maximum(top, best)
        total = jnp.zeros((1, TOK), f32)
        for d in range(REACH + 1):
            e = jnp.exp(scores_ref[d] - top)
            scores_ref[d] = e
            total = total + jnp.sum(e, axis=0, keepdims=True)
        inverse = 1.0 / total
        delta = jnp.zeros((1, TOK), f32)
        for d in range(REACH + 1):
            value_h = v0[:, cols] if d == 0 else near[d - 1][1, :, cols]
            low_p = (scores_ref[d] * inverse).astype(bf16).astype(f32)
            delta = delta + jnp.sum(low_p * nt(value_h, grad_h), axis=0, keepdims=True)
        rows.append((top, inverse, delta))
    for h in range(2):
        for n in range(3):
            stats[3 * h + n : 3 * h + n + 1, :] = rows[h][n]
    stats[6:8, :] = jnp.zeros((2, TOK), f32)


def own_kernel(meta, stats, q, g, k0, v0, b1, b2, b3, b4, dq, dk, dv):
    near = [b1, b2, b3, b4]
    low = meta[1:2, :]
    high = meta[0:1, :]
    for h in range(2):
        cols = head_cols(h)
        query_h = q[:, cols]
        grad_h = g[:, cols]
        top = stats[3 * h : 3 * h + 1, :]
        inverse = stats[3 * h + 1 : 3 * h + 2, :]
        delta = stats[3 * h + 2 : 3 * h + 3, :]
        acc = jnp.zeros((TOK, HD), f32)
        for d in range(REACH + 1):
            key_h = k0[:, cols] if d == 0 else near[d - 1][0, :, cols]
            value_h = v0[:, cols] if d == 0 else near[d - 1][1, :, cols]
            s = masked_scores(key_h, query_h, low, high if d == 0 else None, d * TOK)
            prob = jnp.exp(s - top) * inverse
            ds = (prob * (nt(value_h, grad_h) - delta)).astype(bf16)
            acc = acc + tn(ds, key_h)
            if d == 0:
                dk[:, cols] = nn(ds, query_h)
                dv[:, cols] = nn(prob.astype(bf16), grad_h)
        dq[:, cols] = (acc * scale).astype(bf16)


def later_kernel(
    start, meta, k0, v0, a1, a2, a3, a4, s1, s2, s3, s4, dq, dk, dv, out, image
):
    later = [a1, a2, a3, a4]
    stats = [s1, s2, s3, s4]
    for h in range(2):
        cols = head_cols(h)
        key_h = k0[:, cols]
        value_h = v0[:, cols]
        dkey = dk[:, cols]
        dvalue = dv[:, cols]
        for d in range(1, REACH + 1):
            query_h = later[d - 1][0, :, cols]
            grad_h = later[d - 1][1, :, cols]
            row = stats[d - 1]
            low = meta[1 + d : 2 + d, :]
            s = masked_scores(key_h, query_h, low, None, 0)
            prob = jnp.exp(s - row[3 * h : 3 * h + 1, :]) * row[3 * h + 1 : 3 * h + 2, :]
            ds = (prob * (nt(value_h, grad_h) - row[3 * h + 2 : 3 * h + 3, :])).astype(bf16)
            dkey = dkey + nn(ds, query_h)
            dvalue = dvalue + nn(prob.astype(bf16), grad_h)
        out[1, :, cols] = (dkey * scale).astype(bf16)
        out[2, :, cols] = dvalue.astype(bf16)
    out[0] = dq[...]
    at = start[0]
    row = lax.broadcasted_iota(jnp.int32, (IMGTOK, TOK), 0) + at
    col = lax.broadcasted_iota(jnp.int32, (IMGTOK, TOK), 1)
    pick = jnp.where(row == col, 1.0, 0.0).astype(bf16)
    for n in range(3):
        image[n] = nn(pick, out[n]).astype(bf16)


def paired(flags, own, other):
    first = flags[0] == 0
    return jnp.where(first, own, other), jnp.where(first, other, own)


def patch_kernel(flags, w, own, other, pw, out, acc):
    step = pl.program_id(0)

    @pl.when(step == 0)
    def _():
        acc[...] = jnp.zeros_like(acc)

    for n in range(2):
        t = jnp.zeros((2 * IMGTOK, TOK), f32)
        for p in range(3):
            both = jnp.concatenate(paired(flags, own[p], other[p]), axis=0)
            t = t + nt(both, w[n, :, p].reshape(TOK, TOK))
        acc[...] = acc[...] + nt(t.astype(bf16), pw[n, :PCH])

    @pl.when(step == pl.num_programs(0) - 1)
    def _():
        total = acc[...].astype(bf16)
        for n in range(8):
            out[n] = total


def grad_kernel(flags, w, own, other, out):
    for m in range(2):
        for n in range(2):
            t = jnp.zeros((TOK, TOK), f32)
            for p in range(3):
                t = t + nt(w[m, :, p].reshape(TOK, TOK), paired(flags, own[p], other[p])[n])
            out[m, :, n * TOK : (n + 1) * TOK] = t.astype(bf16)


def conv_kernel(scalars, pieces, k2, slope, left, out):
    head = scalars[0]
    present = scalars[1].astype(f32)
    total = jnp.zeros((IMGTOK, PCH), f32)
    for n in range(pieces.shape[0]):
        total = total + pieces[n].astype(f32)
    incoming = (total * present).astype(bf16)
    q = lax.broadcasted_iota(jnp.int32, (IMGTOK, IMGTOK), 0)
    p = lax.broadcasted_iota(jnp.int32, (IMGTOK, IMGTOK), 1)
    shifts = []
    for o in range(9):
        dr, dc = o // 3 - 1, o % 3 - 1
        hit = ((p >> 3) == (q >> 3) - dr) & ((p & 7) == (q & 7) - dc)
        shifts.append(jnp.where(hit, 1.0, 0.0).astype(bf16))
    dact = jnp.zeros((IMGTOK, 16), f32)
    for o in range(9):
        dact = dact + nt(nn(shifts[o], incoming).astype(bf16), k2[o])
    dpre = (dact * slope[...]).astype(bf16)
    ch = lax.broadcasted_iota(jnp.int32, (PCH, LANES), 0)
    lane = lax.broadcasted_iota(jnp.int32, (PCH, LANES), 1)
    spread = jnp.where((lane < 576) & ((lane & 31) == ch - 32 * head), 1.0, 0.0).astype(bf16)
    ch = lax.broadcasted_iota(jnp.int32, (16, LANES), 0)
    lane = lax.broadcasted_iota(jnp.int32, (16, LANES), 1)
    spread_first = jnp.where((lane >= 576) & ((lane & 15) == ch), 1.0, 0.0).astype(bf16)
    both = (nn(incoming, spread) + nn(dpre, spread_first)).astype(bf16)
    lane = lax.broadcasted_iota(jnp.int32, (IMGTOK, LANES), 1)
    second = jnp.where(lane >= 288, lane - 288, lane) >> 5
    first = (jnp.where(lane >= 720, lane - 720, lane - 576)) >> 4
    which = jnp.where(lane < 576, second, first)
    moved = jnp.zeros((IMGTOK, LANES), f32)
    zero = jnp.zeros((IMGTOK, LANES), bf16)
    for o in range(9):
        moved = moved + nn(shifts[o], jnp.where(which == o, both, zero))
    moved = moved.astype(bf16)
    ends = (0, 288, 576, 720, 864)
    result = jnp.zeros((IMGTOK, LANES), f32)
    for n in range(4):
        part = jnp.where((lane >= ends[n]) & (lane < ends[n + 1]), moved, zero)
        result = result + nn(left[n], part)
    for n in range(7):
        out[:, n, :] = result[:, n * 128 : (n + 1) * 128].astype(bf16)


def whole(space=None):
    return pl.BlockSpec(memory_space=pltpu.VMEM if space is None else space)


def on_chip(kernel, shapes, count, scratch=(), scalars=0):
    return pl.pallas_call(
        kernel,
        out_shape=shapes,
        in_specs=[whole(pltpu.SMEM)] * scalars + [whole()] * (count - scalars),
        out_specs=jax.tree.map(lambda _: whole(), shapes),
        scratch_shapes=list(scratch),
    )


def spec_of(shape, dtype):
    return jax.ShapeDtypeStruct(shape, dtype)


def pick_entry(lookup, wanted):
    return jnp.sum(jnp.where(jnp.arange(lookup.shape[0]) == wanted, lookup, 0))


def passed_along(block, axis, distance):
    devices = range(lax.axis_size(axis))
    route = [(i - distance, i) for i in devices if i - distance in devices]
    return lax.ppermute(block, axis, route)


def swapped(value):
    return lax.ppermute(value, "yl", [(0, 1), (1, 0)])


def once_here(value, reached):
    return lax.optimization_barrier((value, reached))[0]


def exchanged(pieces, axis):
    return lax.all_to_all(pieces, axis, split_axis=0, concat_axis=0, tiled=True)


def sent_to_all(value, axis):
    return exchanged(jnp.broadcast_to(value, (lax.axis_size(axis), *value.shape)), axis)


def adam_update(param, mean, square, grad):
    new_mean = beta_one * mean + (1.0 - beta_one) * grad
    new_square = beta_two * square + (1.0 - beta_two) * grad * grad
    fixed_mean = new_mean / (1.0 - beta_one**adam_step)
    fixed_square = new_square / (1.0 - beta_two**adam_step)
    new_param = param - learn_rate * (
        fixed_mean / (jnp.sqrt(fixed_square) + adam_eps) + decay_rate * param
    )
    return (new_param, new_mean, new_square)


def seen_range(block, doc_lengths, image_count, image_offset):
    index = jnp.arange(doc_lengths.shape[0])
    ends = jnp.sum(jnp.where(index[None, :] <= index[:, None], doc_lengths[None, :], 0), axis=1)
    starts = ends - doc_lengths
    base = block * TOK
    places = base + jnp.arange((REACH + 1) * TOK, dtype=jnp.int32)
    begun = starts[:, None] <= places[None, :]
    low = jnp.max(jnp.where(begun, starts[:, None], 0), axis=0)
    own = places[:TOK]
    over = ends[:, None] > own[None, :]
    doc_end = jnp.min(jnp.where(over, ends[:, None], jnp.int32(1 << 30)), axis=0)
    present = pick_entry(image_count, block)
    offset = pick_entry(image_offset, block)
    local = own - base
    inside = (present > 0) & (local >= offset) & (local < offset + IMGTOK)
    high = jnp.where(
        inside, jnp.maximum(own, jnp.minimum(base + offset + IMGTOK, doc_end) - 1), own
    )
    rows = [high[None], low.reshape(REACH + 1, TOK), jnp.zeros((2, TOK), jnp.int32) + base]
    return jnp.concatenate(rows, axis=0) - base, present, offset


def shards(
    queries,
    keys,
    values,
    out_grad,
    qkv_weight,
    doc_lengths,
    image_count,
    image_offset,
    slab_owner,
    patch_weight,
    conv_input,
    pre_act,
    kernel_first,
    kernel_second,
    mean_first,
    mean_second,
    square_first,
    square_second,
):
    device_index = lax.axis_index(WIDE)
    head_index = lax.axis_index("head")
    side = lax.axis_index("yl")

    before = jnp.stack([keys, values])
    after = jnp.stack([queries, out_grad])
    earlier, later = [], []
    meta, present, offset = seen_range(device_index, doc_lengths, image_count, image_offset)
    for hop in range(REACH):
        before = passed_along(before, WIDE, 1)
        after = passed_along(after, WIDE, -1)
        if hop == REACH - 2:
            before, after, meta = lax.optimization_barrier((before, after, meta))
        else:
            before, after = lax.optimization_barrier((before, after))
        earlier.append(before)
        later.append(after)

    stats = on_chip(
        stats_kernel,
        spec_of((8, TOK), f32),
        9,
        [pltpu.VMEM((REACH + 1, TOK, TOK), f32)],
    )(meta, queries, out_grad, keys, values, *earlier)

    quad = sent_to_all(qkv_weight, "yh")
    quad = once_here(quad, earlier[0])
    weights = lax.all_gather(quad, "z", axis=0)
    slot_rows = jnp.concatenate(
        [conv_input.reshape(PCOLS, CIN), pre_act.reshape(PCOLS, CMID)], axis=1
    )
    slot_rows = jnp.concatenate([slot_rows, kernel_second.astype(bf16)], axis=0)
    along_z = sent_to_all(once_here(slot_rows, quad), "z")
    along_z = once_here(along_z, earlier[1])
    kernel_rows = lax.dynamic_index_in_dim(along_z[:, PCOLS:], head_index, 0, keepdims=False)
    slot_rows = along_z[:, :PCOLS].reshape(64, PCH)
    along_y = jnp.concatenate([slot_rows, kernel_rows], axis=0)
    along_y = sent_to_all(along_y, TALL)
    along_y = once_here(along_y, earlier[2])
    kernel_mine = along_y[:, 64:].reshape(16, 9, PCH).transpose(1, 0, 2)
    slot = pick_entry(slab_owner, device_index)
    my_rows = along_y[:, :64].reshape(8, 8, PCOLS, PCH)
    my_rows = lax.dynamic_slice(
        my_rows, (slot % 8, slot // 8, 0, 0), (1, 1, PCOLS, PCH)
    ).reshape(PCOLS, PCH)
    half_patch = lax.dynamic_index_in_dim(
        patch_weight.reshape(PCH, 4, 2, 64), side, 2, keepdims=False
    ).reshape(PCH, TOK)
    along_head = sent_to_all(jnp.concatenate([half_patch, my_rows], axis=0), "head")
    picture = along_head[:, PCH:].reshape(IMGTOK, CIN + CMID)

    conv_img = picture[:, :CIN]
    pre_img = picture[:, CIN:].astype(f32)
    act = jax.nn.silu(pre_img).astype(bf16)
    left = jnp.concatenate([act.T.reshape(64, 2, 64), conv_img.T.reshape(64, 2, 64)], axis=1)
    left = left.transpose(1, 0, 2)
    sig = jax.nn.sigmoid(pre_img)
    slope = sig * (1.0 + pre_img * (1.0 - sig))
    slope = lax.dynamic_slice_in_dim(slope, head_index * 16, 16, 1)

    stats_later = [passed_along(stats, WIDE, -d) for d in range(1, REACH + 1)]
    dq, dk, dv = on_chip(
        own_kernel,
        (spec_of((TOK, TOK), bf16), spec_of((TOK, TOK), f32), spec_of((TOK, TOK), f32)),
        10,
    )(meta, stats, queries, out_grad, keys, values, *earlier)
    grads, image_grads = on_chip(
        later_kernel,
        (spec_of((3, TOK, TOK), bf16), spec_of((3, IMGTOK, TOK), bf16)),
        15,
        scalars=1,
    )(offset[None], meta, keys, values, *later, *stats_later, dq, dk, dv)

    image_other = swapped(image_grads)
    grads_other = swapped(once_here(grads, image_other))
    flags = side.astype(jnp.int32)[None]

    weight_block = pl.BlockSpec((2, 4, 3, 64, TOK), lambda i: (i, 0, 0, 0, 0))

    def fixed(*shape):
        return pl.BlockSpec(shape, lambda i: (0,) * len(shape))

    pieces = pl.pallas_call(
        patch_kernel,
        out_shape=spec_of((8, 2 * IMGTOK, PCH), bf16),
        grid=(4,),
        in_specs=[
            whole(pltpu.SMEM),
            weight_block,
            fixed(3, IMGTOK, TOK),
            fixed(3, IMGTOK, TOK),
            pl.BlockSpec((2, PCH + PCOLS, TOK), lambda i: (i, 0, 0)),
        ],
        out_specs=fixed(8, 2 * IMGTOK, PCH),
        scratch_shapes=[pltpu.VMEM((2 * IMGTOK, PCH), f32)],
    )(flags, weights, image_grads, image_other, along_head)
    pieces = exchanged(pieces.reshape(16, IMGTOK, PCH), ("head", "yl"))

    present = jnp.stack([head_index.astype(jnp.int32), present.astype(jnp.int32)])
    partial = on_chip(conv_kernel, spec_of((64, 7, 128), bf16), 5, scalars=1)(
        present, pieces, kernel_mine, slope, left
    )

    owned = exchanged(partial, WIDE)

    halves = pl.pallas_call(
        grad_kernel,
        out_shape=spec_of((8, TOK, 2 * TOK), bf16),
        grid=(4,),
        in_specs=[
            whole(pltpu.SMEM),
            weight_block,
            fixed(3, TOK, TOK),
            fixed(3, TOK, TOK),
        ],
        out_specs=pl.BlockSpec((2, TOK, 2 * TOK), lambda i: (i, 0, 0)),
    )(flags, weights, grads, grads_other)
    owned = jnp.sum(once_here(owned, halves).astype(f32), axis=0)
    summed = lax.psum_scatter(halves, "head", scatter_dimension=0)

    squares = jnp.broadcast_to(jnp.sum(owned * owned), (1, 128))
    squares = jnp.sum(sent_to_all(squares, WIDE), axis=0)
    theirs = jnp.where(side == 0, summed[:, TOK:], summed[:, :TOK])
    arrived = swapped(theirs)
    mine = jnp.where(side == 0, summed[:, :TOK], summed[:, TOK:])
    even = jnp.where(side == 0, mine, arrived)
    odd = jnp.where(side == 0, arrived, mine)
    input_grad_t = jnp.stack([even.reshape(4, 64, TOK), odd.reshape(4, 64, TOK)], axis=1)
    input_grad_t = input_grad_t.reshape(512, TOK)

    together = sent_to_all(jnp.concatenate([owned, squares], axis=0), "head")
    total = jnp.sum(together[:, 7, 0])
    columns = together[:, :7].reshape(8, LANES)
    grad_second = (
        columns[:, :576].reshape(8, 2, 9, 32).transpose(1, 2, 0, 3).reshape(18, PCH)
    )
    grad_first = (
        columns[:, 576:864].reshape(8, 2, 9, 16).transpose(1, 2, 0, 3).reshape(18, CMID)
    )
    limit = 0.5 * math.sqrt(9 * CIN * CMID + 9 * CMID * PCH)
    factor = jnp.minimum(1.0, limit / (jnp.sqrt(total) + norm_eps))
    kernel_one, mean_one, square_one = adam_update(
        kernel_first, mean_first, square_first, grad_first * factor
    )
    kernel_two, mean_two, square_two = adam_update(
        kernel_second, mean_second, square_second, grad_second * factor
    )
    return (input_grad_t, kernel_one, kernel_two, mean_one, mean_two, square_one, square_two)


def solution(mesh):
    split = Mesh(mesh.devices.reshape(mesh.shape["head"], 8, 4, 2), ("head", *WIDE))
    placed = (
        P(WIDE, "head"),
        P(WIDE, "head"),
        P(WIDE, "head"),
        P(WIDE, "head"),
        P(None, WIDE, "head"),
        P(),
        P(),
        P(),
        P(),
        P(None, "head"),
        P(WIDE, "head", None, None),
        P(WIDE, "head", None, None),
        P(WIDE, None),
        P(WIDE, None),
        P(WIDE, None),
        P(WIDE, None),
        P(WIDE, None),
        P(WIDE, None),
    )

    return jax.shard_map(
        shards,
        mesh=split,
        in_specs=placed,
        out_specs=(
            P("head", WIDE),
            P(WIDE, None),
            P(WIDE, None),
            P(WIDE, None),
            P(WIDE, None),
            P(WIDE, None),
            P(WIDE, None),
        ),
        check_vma=False,
    )
```

```python
import math

import jax
import jax.numpy as jnp
from jax import lax
from jax.experimental import pallas as pl
from jax.experimental.pallas import tpu as pltpu
from jax.sharding import Mesh
from jax.sharding import PartitionSpec as P


HD = 128
REACH = 4
PCOLS = 8
PCH = 256
CMID = 128
CIN = 128
IMGTOK = 64
TOK = 256
TALL = ("yh", "yl")
WIDE = ("z", *TALL)
LANES = 896

neg_big = -1e30
beta_one = 0.9
beta_two = 0.95
adam_eps = 1e-08
learn_rate = 0.02
decay_rate = 0.1
adam_step = 10
norm_eps = 1e-06
scale = 1.0 / math.sqrt(HD)

f32 = jnp.float32
bf16 = jnp.bfloat16


def nt(a, b):
    return lax.dot_general(a, b, (((1,), (1,)), ((), ())), preferred_element_type=f32)


def nn(a, b):
    return lax.dot_general(a, b, (((1,), (0,)), ((), ())), preferred_element_type=f32)


def tn(a, b):
    return lax.dot_general(a, b, (((0,), (0,)), ((), ())), preferred_element_type=f32)


def head_cols(h):
    return slice(h * HD, (h + 1) * HD)


def masked_scores(key_h, query_h, low, high, shift):
    scores = nt(key_h, query_h) * scale
    place = lax.broadcasted_iota(jnp.int32, scores.shape, 0) - shift
    seen = place >= low
    if high is not None:
        seen = seen & (place <= high)
    return jnp.where(seen, scores, neg_big)


def stats_kernel(meta, q, g, k0, v0, b1, b2, b3, b4, stats, scores_ref):
    near = [b1, b2, b3, b4]
    low = meta[1:2, :]
    high = meta[0:1, :]
    rows = []
    for h in range(2):
        cols = head_cols(h)
        query_h = q[:, cols]
        grad_h = g[:, cols]
        top = None
        for d in range(REACH + 1):
            key_h = k0[:, cols] if d == 0 else near[d - 1][0, :, cols]
            s = masked_scores(key_h, query_h, low, high if d == 0 else None, d * TOK)
            scores_ref[d] = s
            best = jnp.max(s, axis=0, keepdims=True)
            top = best if top is None else jnp.maximum(top, best)
        total = jnp.zeros((1, TOK), f32)
        for d in range(REACH + 1):
            e = jnp.exp(scores_ref[d] - top)
            scores_ref[d] = e
            total = total + jnp.sum(e, axis=0, keepdims=True)
        inverse = 1.0 / total
        delta = jnp.zeros((1, TOK), f32)
        for d in range(REACH + 1):
            value_h = v0[:, cols] if d == 0 else near[d - 1][1, :, cols]
            low_p = (scores_ref[d] * inverse).astype(bf16).astype(f32)
            delta = delta + jnp.sum(low_p * nt(value_h, grad_h), axis=0, keepdims=True)
        rows.append((top, inverse, delta))
    for h in range(2):
        for n in range(3):
            stats[3 * h + n : 3 * h + n + 1, :] = rows[h][n]
    stats[6:8, :] = jnp.zeros((2, TOK), f32)


def own_kernel(meta, stats, q, g, k0, v0, b1, b2, b3, b4, dq, dk, dv):
    near = [b1, b2, b3, b4]
    low = meta[1:2, :]
    high = meta[0:1, :]
    for h in range(2):
        cols = head_cols(h)
        query_h = q[:, cols]
        grad_h = g[:, cols]
        top = stats[3 * h : 3 * h + 1, :]
        inverse = stats[3 * h + 1 : 3 * h + 2, :]
        delta = stats[3 * h + 2 : 3 * h + 3, :]
        acc = jnp.zeros((TOK, HD), f32)
        for d in range(REACH + 1):
            key_h = k0[:, cols] if d == 0 else near[d - 1][0, :, cols]
            value_h = v0[:, cols] if d == 0 else near[d - 1][1, :, cols]
            s = masked_scores(key_h, query_h, low, high if d == 0 else None, d * TOK)
            prob = jnp.exp(s - top) * inverse
            ds = (prob * (nt(value_h, grad_h) - delta)).astype(bf16)
            acc = acc + tn(ds, key_h)
            if d == 0:
                dk[:, cols] = nn(ds, query_h)
                dv[:, cols] = nn(prob.astype(bf16), grad_h)
        dq[:, cols] = (acc * scale).astype(bf16)


def later_kernel(
    start, meta, k0, v0, a1, a2, a3, a4, s1, s2, s3, s4, dq, dk, dv, out, image
):
    later = [a1, a2, a3, a4]
    stats = [s1, s2, s3, s4]
    for h in range(2):
        cols = head_cols(h)
        key_h = k0[:, cols]
        value_h = v0[:, cols]
        dkey = dk[:, cols]
        dvalue = dv[:, cols]
        for d in range(1, REACH + 1):
            query_h = later[d - 1][0, :, cols]
            grad_h = later[d - 1][1, :, cols]
            row = stats[d - 1]
            low = meta[1 + d : 2 + d, :]
            s = masked_scores(key_h, query_h, low, None, 0)
            prob = jnp.exp(s - row[3 * h : 3 * h + 1, :]) * row[3 * h + 1 : 3 * h + 2, :]
            ds = (prob * (nt(value_h, grad_h) - row[3 * h + 2 : 3 * h + 3, :])).astype(bf16)
            dkey = dkey + nn(ds, query_h)
            dvalue = dvalue + nn(prob.astype(bf16), grad_h)
        out[1, :, cols] = (dkey * scale).astype(bf16)
        out[2, :, cols] = dvalue.astype(bf16)
    out[0] = dq[...]
    at = start[0]
    row = lax.broadcasted_iota(jnp.int32, (IMGTOK, TOK), 0) + at
    col = lax.broadcasted_iota(jnp.int32, (IMGTOK, TOK), 1)
    pick = jnp.where(row == col, 1.0, 0.0).astype(bf16)
    for n in range(3):
        image[n] = nn(pick, out[n]).astype(bf16)


def paired(flags, own, other):
    first = flags[0] == 0
    return jnp.where(first, own, other), jnp.where(first, other, own)


def patch_kernel(flags, w, own, other, pw, out, acc):
    step = pl.program_id(0)

    @pl.when(step == 0)
    def _():
        acc[...] = jnp.zeros_like(acc)

    for n in range(2):
        t = jnp.zeros((2 * IMGTOK, TOK), f32)
        for p in range(3):
            both = jnp.concatenate(paired(flags, own[p], other[p]), axis=0)
            t = t + nt(both, w[n, :, p].reshape(TOK, TOK))
        acc[...] = acc[...] + nt(t.astype(bf16), pw[n, :PCH])

    @pl.when(step == pl.num_programs(0) - 1)
    def _():
        total = acc[...].astype(bf16)
        for n in range(8):
            out[n] = total


def grad_kernel(flags, w, own, other, out):
    for m in range(2):
        for n in range(2):
            t = jnp.zeros((TOK, TOK), f32)
            for p in range(3):
                t = t + nt(w[m, :, p].reshape(TOK, TOK), paired(flags, own[p], other[p])[n])
            out[m, :, n * TOK : (n + 1) * TOK] = t.astype(bf16)


def conv_kernel(scalars, pieces, k2, picture, out):
    head = scalars[0]
    present = scalars[1].astype(f32)
    total = jnp.zeros((IMGTOK, PCH), f32)
    for n in range(pieces.shape[0]):
        total = total + pieces[n].astype(f32)
    incoming = (total * present).astype(bf16)
    q = lax.broadcasted_iota(jnp.int32, (IMGTOK, IMGTOK), 0)
    p = lax.broadcasted_iota(jnp.int32, (IMGTOK, IMGTOK), 1)
    shifts = []
    for o in range(9):
        dr, dc = o // 3 - 1, o % 3 - 1
        hit = ((p >> 3) == (q >> 3) - dr) & ((p & 7) == (q & 7) - dc)
        shifts.append(jnp.where(hit, 1.0, 0.0).astype(bf16))
    dact = jnp.zeros((IMGTOK, 16), f32)
    for o in range(9):
        dact = dact + nt(nn(shifts[o], incoming).astype(bf16), k2[o])
    pre = picture[:, CIN:].astype(f32)
    sig = 1.0 / (1.0 + jnp.exp(-pre))
    act = (pre * sig).astype(bf16)
    slope = sig * (1.0 + pre * (1.0 - sig))
    slope = pltpu.roll(slope, (CMID - 16 * head) % CMID, 1)[:, :16]
    dpre = (dact * slope).astype(bf16)
    ch = lax.broadcasted_iota(jnp.int32, (PCH, LANES), 0)
    lane = lax.broadcasted_iota(jnp.int32, (PCH, LANES), 1)
    spread = jnp.where((lane < 576) & ((lane & 31) == ch - 32 * head), 1.0, 0.0).astype(bf16)
    ch = lax.broadcasted_iota(jnp.int32, (16, LANES), 0)
    lane = lax.broadcasted_iota(jnp.int32, (16, LANES), 1)
    spread_first = jnp.where((lane >= 576) & ((lane & 15) == ch), 1.0, 0.0).astype(bf16)
    both = (nn(incoming, spread) + nn(dpre, spread_first)).astype(bf16)
    lane = lax.broadcasted_iota(jnp.int32, (IMGTOK, LANES), 1)
    second = jnp.where(lane >= 288, lane - 288, lane) >> 5
    first = (jnp.where(lane >= 720, lane - 720, lane - 576)) >> 4
    which = jnp.where(lane < 576, second, first)
    moved = jnp.zeros((IMGTOK, LANES), f32)
    zero = jnp.zeros((IMGTOK, LANES), bf16)
    for o in range(9):
        moved = moved + nn(shifts[o], jnp.where(which == o, both, zero))
    moved = moved.astype(bf16)
    ends = (0, 288, 576, 720, 864)
    result = jnp.zeros((IMGTOK, LANES), f32)
    for n in range(4):
        part = jnp.where((lane >= ends[n]) & (lane < ends[n + 1]), moved, zero)
        row = lax.broadcasted_iota(jnp.int32, (64, CMID), 0)
        col = lax.broadcasted_iota(jnp.int32, (64, CMID), 1)
        own = jnp.where(col == 2 * row + n % 2, 1.0, 0.0).astype(bf16)
        source = act if n < 2 else picture[:, :CIN]
        result = result + nn(nt(own, source).astype(bf16), part)
    for n in range(7):
        out[:, n, :] = result[:, n * 128 : (n + 1) * 128].astype(bf16)


def whole(space=None):
    return pl.BlockSpec(memory_space=pltpu.VMEM if space is None else space)


def on_chip(kernel, shapes, count, scratch=(), scalars=0):
    return pl.pallas_call(
        kernel,
        out_shape=shapes,
        in_specs=[whole(pltpu.SMEM)] * scalars + [whole()] * (count - scalars),
        out_specs=jax.tree.map(lambda _: whole(), shapes),
        scratch_shapes=list(scratch),
    )


def spec_of(shape, dtype):
    return jax.ShapeDtypeStruct(shape, dtype)


def pick_entry(lookup, wanted):
    return jnp.sum(jnp.where(jnp.arange(lookup.shape[0]) == wanted, lookup, 0))


def passed_along(block, axis, distance):
    devices = range(lax.axis_size(axis))
    route = [(i - distance, i) for i in devices if i - distance in devices]
    return lax.ppermute(block, axis, route)


def swapped(value):
    return lax.ppermute(value, "yl", [(0, 1), (1, 0)])


def once_here(value, reached):
    return lax.optimization_barrier((value, reached))[0]


def exchanged(pieces, axis):
    return lax.all_to_all(pieces, axis, split_axis=0, concat_axis=0, tiled=True)


def sent_to_all(value, axis):
    return exchanged(jnp.broadcast_to(value, (lax.axis_size(axis), *value.shape)), axis)


def adam_update(param, mean, square, grad):
    new_mean = beta_one * mean + (1.0 - beta_one) * grad
    new_square = beta_two * square + (1.0 - beta_two) * grad * grad
    fixed_mean = new_mean / (1.0 - beta_one**adam_step)
    fixed_square = new_square / (1.0 - beta_two**adam_step)
    new_param = param - learn_rate * (
        fixed_mean / (jnp.sqrt(fixed_square) + adam_eps) + decay_rate * param
    )
    return (new_param, new_mean, new_square)


def seen_range(block, doc_lengths, image_count, image_offset):
    index = jnp.arange(doc_lengths.shape[0])
    ends = jnp.sum(jnp.where(index[None, :] <= index[:, None], doc_lengths[None, :], 0), axis=1)
    starts = ends - doc_lengths
    base = block * TOK
    places = base + jnp.arange((REACH + 1) * TOK, dtype=jnp.int32)
    begun = starts[:, None] <= places[None, :]
    low = jnp.max(jnp.where(begun, starts[:, None], 0), axis=0)
    own = places[:TOK]
    over = ends[:, None] > own[None, :]
    doc_end = jnp.min(jnp.where(over, ends[:, None], jnp.int32(1 << 30)), axis=0)
    present = pick_entry(image_count, block)
    offset = pick_entry(image_offset, block)
    local = own - base
    inside = (present > 0) & (local >= offset) & (local < offset + IMGTOK)
    high = jnp.where(
        inside, jnp.maximum(own, jnp.minimum(base + offset + IMGTOK, doc_end) - 1), own
    )
    rows = [high[None], low.reshape(REACH + 1, TOK), jnp.zeros((2, TOK), jnp.int32) + base]
    return jnp.concatenate(rows, axis=0) - base, present, offset


def shards(
    queries,
    keys,
    values,
    out_grad,
    qkv_weight,
    doc_lengths,
    image_count,
    image_offset,
    slab_owner,
    patch_weight,
    conv_input,
    pre_act,
    kernel_first,
    kernel_second,
    mean_first,
    mean_second,
    square_first,
    square_second,
):
    device_index = lax.axis_index(WIDE)
    head_index = lax.axis_index("head")
    side = lax.axis_index("yl")

    before = jnp.stack([keys, values])
    after = jnp.stack([queries, out_grad])
    earlier, later = [], []
    meta, present, offset = seen_range(device_index, doc_lengths, image_count, image_offset)
    for hop in range(REACH):
        before = passed_along(before, WIDE, 1)
        after = passed_along(after, WIDE, -1)
        if hop == 0:
            before, after, meta = lax.optimization_barrier((before, after, meta))
        else:
            before, after = lax.optimization_barrier((before, after))
        earlier.append(before)
        later.append(after)

    stats = on_chip(
        stats_kernel,
        spec_of((8, TOK), f32),
        9,
        [pltpu.VMEM((REACH + 1, TOK, TOK), f32)],
    )(meta, queries, out_grad, keys, values, *earlier)

    quad = sent_to_all(qkv_weight, "yh")
    quad = once_here(quad, earlier[0])
    weights = lax.all_gather(quad, "z", axis=0)
    slot_rows = jnp.concatenate(
        [conv_input.reshape(PCOLS, CIN), pre_act.reshape(PCOLS, CMID)], axis=1
    )
    slot_rows = jnp.concatenate([slot_rows, kernel_second.astype(bf16)], axis=0)
    along_z = sent_to_all(once_here(slot_rows, quad), "z")
    along_z = once_here(along_z, earlier[1])
    kernel_rows = lax.dynamic_index_in_dim(along_z[:, PCOLS:], head_index, 0, keepdims=False)
    slot_rows = along_z[:, :PCOLS].reshape(64, PCH)
    along_y = jnp.concatenate([slot_rows, kernel_rows], axis=0)
    along_y = sent_to_all(along_y, TALL)
    along_y = once_here(along_y, earlier[2])
    kernel_mine = along_y[:, 64:].reshape(16, 9, PCH).transpose(1, 0, 2)
    slot = pick_entry(slab_owner, device_index)
    my_rows = along_y[:, :64].reshape(8, 8, PCOLS, PCH)
    my_rows = lax.dynamic_slice(
        my_rows, (slot % 8, slot // 8, 0, 0), (1, 1, PCOLS, PCH)
    ).reshape(PCOLS, PCH)
    half_patch = lax.dynamic_index_in_dim(
        patch_weight.reshape(PCH, 4, 2, 64), side, 2, keepdims=False
    ).reshape(PCH, TOK)
    along_head = sent_to_all(jnp.concatenate([half_patch, my_rows], axis=0), "head")
    picture = along_head[:, PCH:].reshape(IMGTOK, CIN + CMID)

    stats_later = [passed_along(stats, WIDE, -d) for d in range(1, REACH + 1)]
    dq, dk, dv = on_chip(
        own_kernel,
        (spec_of((TOK, TOK), bf16), spec_of((TOK, TOK), f32), spec_of((TOK, TOK), f32)),
        10,
    )(meta, stats, queries, out_grad, keys, values, *earlier)
    grads, image_grads = on_chip(
        later_kernel,
        (spec_of((3, TOK, TOK), bf16), spec_of((3, IMGTOK, TOK), bf16)),
        15,
        scalars=1,
    )(offset[None], meta, keys, values, *later, *stats_later, dq, dk, dv)

    image_other = swapped(image_grads)
    grads_other = swapped(once_here(grads, image_other))
    flags = side.astype(jnp.int32)[None]

    weight_block = pl.BlockSpec((2, 4, 3, 64, TOK), lambda i: (i, 0, 0, 0, 0))

    def fixed(*shape):
        return pl.BlockSpec(shape, lambda i: (0,) * len(shape))

    pieces = pl.pallas_call(
        patch_kernel,
        out_shape=spec_of((8, 2 * IMGTOK, PCH), bf16),
        grid=(4,),
        in_specs=[
            whole(pltpu.SMEM),
            weight_block,
            fixed(3, IMGTOK, TOK),
            fixed(3, IMGTOK, TOK),
            pl.BlockSpec((2, PCH + PCOLS, TOK), lambda i: (i, 0, 0)),
        ],
        out_specs=fixed(8, 2 * IMGTOK, PCH),
        scratch_shapes=[pltpu.VMEM((2 * IMGTOK, PCH), f32)],
    )(flags, weights, image_grads, image_other, along_head)
    pieces = exchanged(pieces.reshape(16, IMGTOK, PCH), ("head", "yl"))

    present = jnp.stack([head_index.astype(jnp.int32), present.astype(jnp.int32)])
    partial = on_chip(conv_kernel, spec_of((64, 7, 128), bf16), 4, scalars=1)(
        present, pieces, kernel_mine, picture
    )

    owned = exchanged(partial, WIDE)

    halves = pl.pallas_call(
        grad_kernel,
        out_shape=spec_of((8, TOK, 2 * TOK), bf16),
        grid=(4,),
        in_specs=[
            whole(pltpu.SMEM),
            weight_block,
            fixed(3, TOK, TOK),
            fixed(3, TOK, TOK),
        ],
        out_specs=pl.BlockSpec((2, TOK, 2 * TOK), lambda i: (i, 0, 0)),
    )(flags, weights, grads, grads_other)
    owned = jnp.sum(once_here(owned, halves).astype(f32), axis=0)
    summed = lax.psum_scatter(halves, "head", scatter_dimension=0)

    squares = jnp.broadcast_to(jnp.sum(owned * owned), (1, 128))
    squares = jnp.sum(sent_to_all(squares, WIDE), axis=0)
    theirs = jnp.where(side == 0, summed[:, TOK:], summed[:, :TOK])
    arrived = swapped(theirs)
    mine = jnp.where(side == 0, summed[:, :TOK], summed[:, TOK:])
    even = jnp.where(side == 0, mine, arrived)
    odd = jnp.where(side == 0, arrived, mine)
    input_grad_t = jnp.stack([even.reshape(4, 64, TOK), odd.reshape(4, 64, TOK)], axis=1)
    input_grad_t = input_grad_t.reshape(512, TOK)

    together = sent_to_all(jnp.concatenate([owned, squares], axis=0), "head")
    total = jnp.sum(together[:, 7, 0])
    columns = together[:, :7].reshape(8, LANES)
    grad_second = (
        columns[:, :576].reshape(8, 2, 9, 32).transpose(1, 2, 0, 3).reshape(18, PCH)
    )
    grad_first = (
        columns[:, 576:864].reshape(8, 2, 9, 16).transpose(1, 2, 0, 3).reshape(18, CMID)
    )
    limit = 0.5 * math.sqrt(9 * CIN * CMID + 9 * CMID * PCH)
    factor = jnp.minimum(1.0, limit / (jnp.sqrt(total) + norm_eps))
    kernel_one, mean_one, square_one = adam_update(
        kernel_first, mean_first, square_first, grad_first * factor
    )
    kernel_two, mean_two, square_two = adam_update(
        kernel_second, mean_second, square_second, grad_second * factor
    )
    return (input_grad_t, kernel_one, kernel_two, mean_one, mean_two, square_one, square_two)


def solution(mesh):
    split = Mesh(mesh.devices.reshape(mesh.shape["head"], 8, 4, 2), ("head", *WIDE))
    placed = (
        P(WIDE, "head"),
        P(WIDE, "head"),
        P(WIDE, "head"),
        P(WIDE, "head"),
        P(None, WIDE, "head"),
        P(),
        P(),
        P(),
        P(),
        P(None, "head"),
        P(WIDE, "head", None, None),
        P(WIDE, "head", None, None),
        P(WIDE, None),
        P(WIDE, None),
        P(WIDE, None),
        P(WIDE, None),
        P(WIDE, None),
        P(WIDE, None),
    )

    return jax.shard_map(
        shards,
        mesh=split,
        in_specs=placed,
        out_specs=(
            P("head", WIDE),
            P(WIDE, None),
            P(WIDE, None),
            P(WIDE, None),
            P(WIDE, None),
            P(WIDE, None),
            P(WIDE, None),
        ),
        check_vma=False,
    )
```
